256 devices in a mesh: list: 32 (over x, y, core), rep: 8 (over z).
Axes of the slice: x: 4, y: 4, z: 8, core: 2. Of those that a mesh axis runs over, the one named last changes fastest.
Arguments:
- memory_rows: bfloat16 [65536, 1024], P(('list', 'rep'))
- list_owner: int32 [65536, 1], P(('list', 'rep')), may hold values from 0 to 31; in each aligned block of 256 rows (0 to 255, 256 to 511, ...) at most 32 rows name the same one
- list_slot: int32 [65536], P(('list', 'rep')), may hold values from 0 to 2047
- pq_codes: int32 [65536, 16], P(('list', 'rep')), may hold values from 0 to 255
- valid_rows: int32 [256], P(('list', 'rep')), may hold values from 128 to 256
- centroids: bfloat16 [65536, 1024], P('list'), may hold values from -3 to 3
- codebook: float32 [16, 256, 64], replicated
Outputs:
- new_codebook: float32 [16, 256, 64], P('rep')
- row_error: float32 [65536], P(('list', 'rep'))
The draws below stay inside these ranges and needn't reach their ends.
Inputs may be any that keep to these rules, and one draw needn't show every extreme that they name: `list_owner`: the rows of one device name one index of list at most 32 times, and some device's rows name one exactly 32 times.
All inputs are finite; a program needn't handle non-finite values.
Results may differ from the reference program's by a relative error of at most 0.0038.
Values may be sent and summed in bfloat16 or wider, within the bound.
A program may use at most 128 MiB of HBM per device.

```python
import math
import jax
import jax.numpy as jnp
import numpy as np
from jax import lax

D = 1024
M = 16
K = 256
DS = 64
ROWS_DEV = 256
LIST_DEV = 2048
CAP = 32
ROWS = 65536
LISTS = 65536
N_LIST = 32
DEVICES = 256


def shared_codes(key):
    uniform_codes = jax.random.randint(jax.random.fold_in(key, 11), (ROWS, M), 0, K, dtype=jnp.int32)
    offsets = jax.random.randint(jax.random.fold_in(key, 14), (M,), 0, K, dtype=jnp.int32)
    block_ids = jnp.arange(ROWS, dtype=jnp.int32) // ROWS_DEV
    favoured = (block_ids[:, None] + offsets[None, :]) % K
    pick = jax.random.randint(jax.random.fold_in(key, 15), (ROWS, M), 0, 2, dtype=jnp.int32)
    return jnp.where(pick == 1, favoured, uniform_codes).astype(jnp.int32)


def shared_book(key):
    return jax.random.normal(jax.random.fold_in(key, 12), (M, K, DS), jnp.float32)


def draw_pq_codes(key, part):
    return shared_codes(key)


def draw_codebook(key, part):
    return shared_book(key)


def draw_memory_rows(key, part):
    codes_drawn = shared_codes(key)
    book = shared_book(key)
    recon = book[jnp.arange(M)[None, :], codes_drawn].reshape(ROWS, D)
    noise_key = jax.random.fold_in(key, 13)
    block_bias = jax.random.normal(jax.random.fold_in(key, 16), (ROWS // ROWS_DEV, D), jnp.float32)
    bias_rows = jnp.repeat(block_bias, ROWS_DEV, axis=0)
    noise = 0.5 * jax.random.normal(noise_key, (ROWS, D), jnp.float32)
    return (recon + noise + bias_rows).astype(jnp.bfloat16)


def place_ends(result, own_key, least, largest):
    shape = result.shape
    index_at = [jax.random.randint(jax.random.fold_in(own_key, axis), (), 0, shape[axis]) for axis in range(len(shape))]
    result = result.at[tuple(index_at)].set(least)
    longest = shape.index(max(shape))
    index_at[longest] = (index_at[longest] + 1) % shape[longest]
    return result.at[tuple(index_at)].set(largest)


def block_levels(rng, dims, split, smallest, high):
    level = 1.0
    for position, blocks in split:
        heights = jax.random.uniform(jax.random.fold_in(jax.random.fold_in(rng, 6), position), (blocks,), jnp.float32, smallest / len(split), high / len(split))
        level = level * jnp.repeat(jnp.exp(heights), dims[position] // blocks).reshape((-1,) + (1,) * (len(dims) - 1 - position))
    return level


def deal_out(rng, own, number, rows, amount, top, most, lean):
    sequence = jax.random.permutation(rng, amount)
    packed, common = portions_of(amount, rows * top, most, lean, True), portions_of(amount, rows * top, most, lean, False)
    places = jnp.arange(amount)

    def named(sizes, rotation):
        used = int((sizes > 0).sum())
        fixed = max(1, used // 4)
        shifted = fixed + (places - fixed + rotation * (used - fixed)) % max(1, amount - fixed)
        return jnp.zeros((amount,), jnp.int32).at[sequence[jnp.where(places < fixed, places, shifted)]].set(jnp.asarray(sizes, jnp.int32))

    sizes = jnp.where(number % 4 == 0, named(packed, number // 4), named(common, number - number // 4 - 1))
    mixed = jax.random.permutation(jax.random.fold_in(own, 3), amount)
    source_of, taker = mixed[0:amount // 2 * 2:2], mixed[1:amount // 2 * 2:2]
    slack = jnp.minimum(sizes[source_of] - 1, most - sizes[taker]) // 2
    slack = jnp.where((source_of == sequence[0]) | (taker == sequence[0]) | (sizes[taker] == 0), 0, jnp.maximum(slack, 0))
    shifted = jax.random.randint(jax.random.fold_in(own, 4), (amount // 2,), 0, 1 << 20) % (slack + 1)
    sizes = sizes.at[source_of].add(-shifted).at[taker].add(shifted)
    labels = jnp.searchsorted(jnp.cumsum(sizes), jnp.arange(rows * top), side="right").astype(jnp.int32)
    listing = labels.reshape(top, rows).T
    listing = listing[jax.random.permutation(jax.random.fold_in(own, 1), rows)]
    rotation = jax.random.randint(jax.random.fold_in(own, 2), (rows, 1), 0, top)
    return jnp.take_along_axis(listing, (jnp.arange(top)[None, :] + rotation) % top, axis=1)


def portions_of(count, total, limit, skew, full):
    portions = [(1 << 20) // math.isqrt(rank ** skew) + 1 for rank in range(1, count + 1)]
    largest = limit if full else min(limit, max(-(-total // count), total * portions[0] // sum(portions)))
    least = 1 if total - largest >= count - 1 else 0
    given, spare = [largest] + [least] * (count - 1), total - largest - least * (count - 1)
    while spare > 0:
        candidates = [i for i in range(1, count) if given[i] < largest] or [i for i in range(1, count) if given[i] < limit]
        whole, remaining = sum([portions[i] for i in candidates]), spare
        for i in candidates:
            addition = min(limit - given[i], max(1, remaining * portions[i] // whole), spare)
            given[i] = given[i] + addition
            spare = spare - addition
    return np.array(given)


def centred(own_key, extent, width, most, shards=(), kind=jnp.bfloat16):
    array = width * jax.random.normal(own_key, extent, jnp.float32)
    if shards:
        array = array * block_levels(own_key, extent, shards, -0.22, 0.18)
    return jnp.clip(array, -most, most).astype(kind)


def setup_inputs(seed: int = 0) -> dict:
    key_list = jax.random.split(jax.random.key(seed), 8)
    memory_rows = draw_memory_rows(jax.random.fold_in(key_list[7], 71), 0)
    list_owner_keys = jax.random.split(jax.random.fold_in(key_list[1], 1), ROWS // ROWS_DEV)
    list_owner_turns = jax.random.permutation(jax.random.fold_in(key_list[1], 3), ROWS // ROWS_DEV)
    list_owner = jax.vmap(lambda own, number: deal_out(jax.random.fold_in(key_list[1], 2), own, number, ROWS_DEV, N_LIST, 1, CAP, 2))(list_owner_keys, list_owner_turns).reshape((ROWS, 1))
    list_slot = place_ends(jax.random.randint(key_list[2], (ROWS,), 0, LIST_DEV), jax.random.fold_in(key_list[2], 1), 0, LIST_DEV - 1).astype(jnp.int32)
    pq_codes = draw_pq_codes(jax.random.fold_in(key_list[7], 71), 0)
    valid_rows = place_ends(jax.random.randint(key_list[4], (DEVICES,), ROWS_DEV // 2, ROWS_DEV + 1), jax.random.fold_in(key_list[4], 1), ROWS_DEV // 2, ROWS_DEV).astype(jnp.int32)
    centroids = centred(key_list[5], (LISTS, D), 0.5, 3.0, ((0, 32),))
    codebook = draw_codebook(jax.random.fold_in(key_list[7], 71), 0)
    return {"memory_rows": memory_rows, "list_owner": list_owner, "list_slot": list_slot, "pq_codes": pq_codes, "valid_rows": valid_rows, "centroids": centroids, "codebook": codebook}


prior_weight = 4.0


def block_terms(block_rows, block_owner, block_slot, block_codes, count, centroids, codebook):
    is_live = jnp.arange(ROWS_DEV).astype(jnp.int32) < count
    list_index = (block_owner[:, 0] * LIST_DEV + block_slot).astype(jnp.int32)
    centre = centroids[list_index].astype(jnp.float32)
    residual = jnp.where(is_live[:, None], block_rows.astype(jnp.float32) - centre, 0.0)
    subspace = jnp.arange(M).astype(jnp.int32)
    recon = codebook[subspace[None, :], block_codes].reshape(ROWS_DEV, D)
    row_error = jnp.where(is_live, jnp.mean((residual - recon) ** 2, axis=1), 0.0)
    rounded = lax.optimization_barrier(residual.astype(jnp.bfloat16)).astype(jnp.float32)
    flat_ids = (subspace[None, :] * K + block_codes).astype(jnp.int32).reshape(-1)
    sums = jax.ops.segment_sum(rounded.reshape(ROWS_DEV * M, DS), flat_ids, M * K).reshape(M, K, DS)
    live_float = jnp.repeat(is_live.astype(jnp.float32), M)
    counts = jax.ops.segment_sum(live_float, flat_ids, M * K).reshape(M, K)
    return row_error, sums, counts


def reference(memory_rows, list_owner, list_slot, pq_codes, valid_rows, centroids, codebook):
    blocks = ROWS // ROWS_DEV
    inputs = (memory_rows.reshape(blocks, ROWS_DEV, D), list_owner.reshape(blocks, ROWS_DEV, 1),
              list_slot.reshape(blocks, ROWS_DEV), pq_codes.reshape(blocks, ROWS_DEV, M), valid_rows)

    def step(carry, item):
        row_error, sums, counts = block_terms(item[0], item[1], item[2], item[3], item[4], centroids, codebook)
        return (carry[0] + sums, carry[1] + counts), row_error

    start = (jnp.zeros((M, K, DS), jnp.float32), jnp.zeros((M, K), jnp.float32))
    totals, errors = lax.scan(step, start, inputs)
    new_codebook = (totals[0] + prior_weight * codebook) / (totals[1][:, :, None] + prior_weight)
    return new_codebook, errors.reshape(ROWS)
```

```python
import functools

import jax
import jax.numpy as jnp
from jax import lax
from jax.experimental import pallas as pl
from jax.experimental.pallas import tpu as pltpu
from jax.sharding import PartitionSpec as P

prior_weight = 4.0

D = 1024
M = 16
K = 256
DS = 64
ROWS = 256
LISTS = 2048
CAP = 32
NL = 32
NZ = 8
SLOTS = NL * CAP
CW = 128
STEPS = D // CW

F32 = jnp.float32
BF16 = jnp.bfloat16
MESH = pl.DeviceIdType.MESH


def iota(shape, axis):
    return lax.broadcasted_iota(jnp.int32, shape, axis)


def dot(a, b, ca, cb):
    return lax.dot_general(a, b, (((ca,), (cb,)), ((), ())), preferred_element_type=F32)


def onehot(mask):
    return jnp.where(mask, 1.0, 0.0).astype(BF16)


def kernel(
    valid,
    owner,
    slot,
    codes,
    rows_hbm,
    cent_hbm,
    cb_hbm,
    newcb,
    err_out,
    rows,
    cents,
    cb,
    cbd,
    place,
    pos_ref,
    mt_send,
    mt_recv,
    meta,
    pick,
    send,
    recv,
    cent,
    recon,
    ohc,
    err,
    ring_in,
    ring_out,
    cz_send,
    cz_recv,
    cx_send,
    cx_recv,
    rs_send,
    rs_recv,
    ag_send,
    ag_recv,
    et_send,
    et_recv,
    local_sem,
    meta_sem,
    data_ss,
    data_rs,
    ring_ss,
    ring_rs,
    cz_sem,
    cx_sem,
    rs_sem,
    ag_sem,
    et_sem,
):
    me = lax.axis_index("list")
    z = lax.axis_index("rep")

    load_rows = pltpu.make_async_copy(rows_hbm, rows, local_sem.at[0])
    load_cb = pltpu.make_async_copy(cb_hbm, cb, local_sem.at[1])
    load_cents = pltpu.make_async_copy(cent_hbm, cents, local_sem.at[2])
    load_rows.start()
    load_cb.start()
    load_cents.start()

    barrier = pltpu.get_barrier_semaphore()

    def greet(k, c):
        pl.semaphore_signal(
            barrier, inc=1, device_id=(lax.rem(me + k, NL), z), device_id_type=MESH
        )
        return c

    def greet_z(k, c):
        pl.semaphore_signal(
            barrier, inc=1, device_id=(me, lax.rem(z + k, NZ)), device_id_type=MESH
        )
        return c

    lax.fori_loop(1, NL, greet, 0)
    lax.fori_loop(1, NZ, greet_z, 0)

    def peer(k):
        return lax.rem(me + k, NL)

    def copy_to(src, dst, ssem, rsem, who, plane):
        return pltpu.make_async_remote_copy(
            src_ref=src,
            dst_ref=dst,
            send_sem=ssem,
            recv_sem=rsem,
            device_id=(who, plane),
            device_id_type=MESH,
        )

    def pair_at(s):
        return lax.rem(z + (NZ - 1) - s, NZ)

    def column(s):
        return pl.multiple_of(pair_at(s) * CW, CW)

    live = iota((1, ROWS), 1) < valid[0]
    own = jnp.where(live, owner[...], NL)
    named = iota((NL, ROWS), 0) == own
    named_f = jnp.where(named, 1.0, 0.0)
    earlier = onehot(iota((ROWS, ROWS), 0) < iota((ROWS, ROWS), 1))
    before = dot(named_f.astype(BF16), earlier, 1, 0)
    rank = jnp.sum(before * named_f, axis=0, keepdims=True)
    pos = jnp.where(live, own.astype(F32) * CAP + rank, -1.0)
    pos_ref[...] = pos

    def quarter(q):
        i = iota((ROWS, ROWS), 0)
        return ((i // 8) * CAP + q * 8 + i % 8).astype(F32)

    codes_f = jnp.where(live, (codes[...] + 1).astype(F32), 0.0)
    low = (slot[...] % 256).astype(F32)
    high = (slot[...] // 256 + 1).astype(F32)
    which = iota((16, ROWS), 0)
    tail = jnp.where(which == 0, low, jnp.where(which == 1, high, 0.0))
    tail = jnp.where(live, tail, 0.0)
    meta_t = jnp.concatenate([codes_f, tail], axis=0).astype(BF16)
    blank = jnp.zeros((32, ROWS), BF16)
    packed = jnp.zeros((ROWS, 128), F32)
    for q in range(4):
        shifted = jnp.concatenate([meta_t if i == q else blank for i in range(4)], axis=0)
        packed += dot(onehot(quarter(q) == pos), shifted, 1, 1)
    mt_send[...] = packed
    for b in range(4):
        place[pl.ds(b * 256, 256), :] = onehot((iota((256, ROWS), 0) + b * 256).astype(F32) == pos)

    ring_in[0] = jnp.zeros((2, DS, K), F32)
    err[...] = jnp.zeros((SLOTS, CW), F32)

    pl.semaphore_wait(barrier, NL - 1 + NZ - 1)

    def tile8(j):
        return pl.ds(pl.multiple_of(j * 8, 8), 8)

    def tile32(j):
        return pl.ds(pl.multiple_of(j * CAP, CAP), CAP)

    def send_meta(k, c):
        j = peer(k)
        copy_to(mt_send.at[tile8(j)], mt_recv.at[tile8(me)], meta_sem.at[0], meta_sem.at[1], j, z).start()
        return c

    lax.fori_loop(1, NL, send_meta, 0)
    mt_recv[tile8(me), :] = mt_send[tile8(me), :]

    load_rows.wait()

    def bucket_and_send(first):
        both = jnp.concatenate(
            [rows[:, pl.ds(column(first), CW)], rows[:, pl.ds(column(first + 1), CW)]], axis=1
        )
        for b in range(4):
            part = dot(place[pl.ds(b * 256, 256), :], both, 1, 0).astype(BF16)
            send[first, pl.ds(b * 256, 256), :] = part[:, :CW]
            send[first + 1, pl.ds(b * 256, 256), :] = part[:, CW:]
        for h in range(2):
            c = first + h
            for k in range(1, NL):
                j = peer(k)
                copy_to(
                    send.at[c, tile32(j)], recv.at[c, tile32(me)], data_ss.at[c], data_rs.at[c], j, z
                ).start()
            recv[c, tile32(me), :] = send[c, tile32(me), :]

    bucket_and_send(0)

    eye = onehot(iota((ROWS, ROWS), 0) == iota((ROWS, ROWS), 1))
    natural = dot(eye, meta_t, 1, 1)
    code_lane = (iota((ROWS, K), 1) + 1).astype(F32)
    ones = jnp.ones((16, ROWS), BF16)
    for m in range(M):
        tally = dot(ones, onehot(natural[:, m : m + 1] == code_lane), 1, 0)
        for h in range(2):
            cz_send[m // 2, (m % 2) * 2 + h] = tally[0:1, h * 128 : (h + 1) * 128]

    def send_cz(k, c):
        other = lax.rem(z + k, NZ)
        copy_to(cz_send.at[other], cz_recv.at[z], cz_sem.at[0], cz_sem.at[1], me, other).start()
        return c

    lax.fori_loop(1, NZ, send_cz, 0)
    cz_recv[z] = cz_send[z]

    bucket_and_send(2)

    load_cb.wait()
    for p in range(STEPS):
        none = jnp.zeros((DS, K), F32)
        top = jnp.concatenate([cb[2 * p], none], axis=1)
        bottom = jnp.concatenate([none, cb[2 * p + 1]], axis=1)
        block = jnp.concatenate([top, bottom], axis=0)
        coarse = block.astype(BF16)
        cbd[p, 0:CW, :] = coarse
        cbd[p, CW : 2 * CW, :] = (block - coarse.astype(F32)).astype(BF16)

    copy_to(
        cz_send.at[pl.ds(0, NZ - 1)], cz_recv.at[pl.ds(0, NZ - 1)], cz_sem.at[0], cz_sem.at[1], me, z
    ).wait_recv()
    cx_send[...] = jnp.sum(cz_recv[...], axis=0)

    def send_cx(k, c):
        j = peer(k)
        piece = (j // 16) * 2 + lax.rem(j, 2)
        copy_to(cx_send.at[piece], cx_recv.at[me], cx_sem.at[0], cx_sem.at[1], j, z).start()
        return c

    lax.fori_loop(1, NL, send_cx, 0)
    cx_recv[me] = cx_send[(me // 16) * 2 + lax.rem(me, 2)]

    copy_to(
        mt_send.at[pl.ds(0, 248)], mt_recv.at[pl.ds(0, 248)], meta_sem.at[0], meta_sem.at[1], me, z
    ).wait_recv()
    got = mt_recv[...]
    for q in range(4):
        turned = got if q == 0 else pltpu.roll(got, 128 - 32 * q, 1)
        meta[:, q] = turned.reshape(NL, 8, 128)

    def meta_rows(b):
        return meta[pl.ds(b * 8, 8)].reshape(256, 128)

    def build_pick(b, c):
        m = meta_rows(b)
        wanted = m[:, 17:18] * 256.0 + m[:, 16:17] - 256.0
        for t in range(4):
            lanes = (iota((256, 512), 1) + t * 512).astype(F32)
            pick[pl.ds(b * 256, 256), t * 512 : (t + 1) * 512] = onehot(wanted == lanes)
        return c

    lax.fori_loop(0, 4, build_pick, 0)
    load_cents.wait()

    def two_steps(u, carry):
        @pl.when(u < 2)
        def _():
            bucket_and_send(2 * u + 4)

        table = jnp.concatenate(
            [cents[:, pl.ds(column(2 * u), CW)], cents[:, pl.ds(column(2 * u + 1), CW)]], axis=1
        )

        def ahead(b, c):
            r = pl.ds(b * 256, 256)
            centre = dot(pick[r, :], table, 1, 0)
            m = meta_rows(b)
            for h in range(2):
                p = pair_at(2 * u + h)
                cent[h, r, :] = centre[:, h * CW : (h + 1) * CW]
                turned = pltpu.roll(m, lax.rem(128 - 2 * p, 128), 1)
                hot = jnp.concatenate(
                    [onehot(turned[:, 0:1] == code_lane), onehot(turned[:, 1:2] == code_lane)], axis=1
                )
                ohc[h, r, :] = hot
                value = dot(hot, cbd[p], 1, 1)
                recon[h, r, :] = value[:, :CW] + value[:, CW:]
            return c

        lax.fori_loop(0, 4, ahead, 0)

        for h in range(2):
            s = 2 * u + h
            copy_to(
                send.at[s, pl.ds(0, SLOTS - CAP)],
                recv.at[s, pl.ds(0, SLOTS - CAP)],
                data_ss.at[s],
                data_rs.at[s],
                me,
                z,
            ).wait_recv()

            total = jnp.zeros((CW, 2 * K), F32)
            for b in range(4):
                r = pl.ds(b * 256, 256)
                residual = recv[s, r, :].astype(F32) - cent[h, r, :]
                gap = residual - recon[h, r, :]
                err[r, :] += gap * gap
                total += dot(residual.astype(BF16), ohc[h, r, :], 0, 0)
            for a in range(2):
                mine = total[a * DS : (a + 1) * DS, a * K : (a + 1) * K]
                hop = copy_to(
                    ring_out.at[s, a],
                    ring_in.at[lax.rem(s + 1, STEPS), a],
                    ring_ss.at[s, a],
                    ring_rs.at[lax.rem(s + 1, STEPS), a],
                    me,
                    lax.rem(z + 1, NZ),
                )
                arrived = copy_to(
                    ring_out.at[s, a], ring_in.at[s, a], ring_ss.at[s, a], ring_rs.at[s, a], me, z
                )
                if h == 0:
                    pl.when(u > 0)(arrived.wait_recv)
                else:
                    arrived.wait_recv()
                ring_out[s, a] = mine + ring_in[s, a]
                if h == 0:
                    hop.start()
                else:
                    pl.when(u < 3)(hop.start)
        return carry

    lax.fori_loop(0, STEPS // 2, two_steps, 0)

    for a in range(2):
        for d in range(8):
            for h in range(2):
                rs_send[a * 16 + d * 2 + h] = ring_out[
                    STEPS - 1, a, d * 8 : (d + 1) * 8, h * 128 : (h + 1) * 128
                ]

    def send_rs(k, c):
        j = peer(k)
        copy_to(rs_send.at[j], rs_recv.at[me], rs_sem.at[0], rs_sem.at[1], j, z).start()
        return c

    lax.fori_loop(1, NL, send_rs, 0)
    rs_recv[me] = rs_send[me]

    summed = (jnp.sum(err[...], axis=1, keepdims=True) * (1.0 / D)).reshape(NL, 4, 8, 1)
    group = iota((NL, 8, 128), 2) // 32
    tiles = jnp.zeros((NL, 8, 128), F32)
    for q in range(4):
        tiles = jnp.where(group == q, summed[:, q], tiles)
    et_send[...] = tiles.reshape(NL * 8, 128)

    def send_et(k, c):
        j = peer(k)
        copy_to(et_send.at[tile8(j)], et_recv.at[tile8(me)], et_sem.at[0], et_sem.at[1], j, z).start()
        return c

    lax.fori_loop(1, NL, send_et, 0)
    et_recv[tile8(me), :] = et_send[tile8(me), :]

    def wait_all(src, dst, sem):
        whole = copy_to(src, dst, sem.at[0], sem.at[1], me, z)
        return whole

    first31 = pl.ds(0, NL - 1)
    cx_all = wait_all(cx_recv.at[first31], cx_recv.at[first31], cx_sem)
    rs_all = wait_all(rs_send.at[first31], rs_recv.at[first31], rs_sem)
    ag_all = wait_all(ag_recv.at[first31], ag_recv.at[first31], ag_sem)
    et_all = wait_all(et_send.at[pl.ds(0, 248)], et_recv.at[pl.ds(0, 248)], et_sem)

    cx_all.wait_recv()
    count = jnp.sum(cx_recv[...], axis=0)
    rs_all.wait_recv()
    total = jnp.sum(rs_recv[...], axis=0)
    old = cb[
        2 * z + me // 16,
        pl.ds(pl.multiple_of(lax.rem(me // 2, 8) * 8, 8), 8),
        pl.ds(pl.multiple_of(lax.rem(me, 2) * 128, 128), 128),
    ]
    ag_send[...] = (total + prior_weight * old) / (count + prior_weight)

    def send_ag(k, c):
        j = peer(k)
        copy_to(ag_send, ag_recv.at[me], ag_sem.at[0], ag_sem.at[1], j, z).start()
        return c

    lax.fori_loop(1, NL, send_ag, 0)
    ag_recv[me] = ag_send[...]

    et_all.wait_recv()
    final = jnp.zeros((1, ROWS), F32)
    where = pos_ref[...]
    for q in range(4):
        e = et_recv[:, q * 32 : q * 32 + 1]
        final += jnp.sum(jnp.where(quarter(q) == where, e, 0.0), axis=0, keepdims=True)
    err_out[...] = final

    ag_all.wait_recv()
    for a in range(2):
        for d in range(8):
            for h in range(2):
                newcb[a, d * 8 : (d + 1) * 8, h * 128 : (h + 1) * 128] = ag_recv[a * 16 + d * 2 + h]

    copy_to(
        mt_send.at[pl.ds(0, 248)], mt_recv.at[pl.ds(0, 248)], meta_sem.at[0], meta_sem.at[1], me, z
    ).wait_send()
    copy_to(
        cz_send.at[pl.ds(0, NZ - 1)], cz_recv.at[pl.ds(0, NZ - 1)], cz_sem.at[0], cz_sem.at[1], me, z
    ).wait_send()

    def drain(s, c):
        copy_to(
            send.at[s, pl.ds(0, SLOTS - CAP)],
            recv.at[s, pl.ds(0, SLOTS - CAP)],
            data_ss.at[s],
            data_rs.at[s],
            me,
            z,
        ).wait_send()
        return c

    lax.fori_loop(0, STEPS, drain, 0)

    def drain_ring(s, c):
        for a in range(2):
            copy_to(
                ring_out.at[s, a], ring_in.at[s, a], ring_ss.at[s, a], ring_rs.at[s, a], me, z
            ).wait_send()
        return c

    lax.fori_loop(0, STEPS - 1, drain_ring, 0)
    cx_all.wait_send()
    rs_all.wait_send()
    et_all.wait_send()
    ag_all.wait_send()


def body(memory_rows, list_owner, list_slot, pq_codes, valid_rows, centroids, codebook):
    vmem = pl.BlockSpec(memory_space=pltpu.VMEM)
    anywhere = pl.BlockSpec(memory_space=pl.ANY)
    dma = pltpu.SemaphoreType.DMA
    newcb, err = pl.pallas_call(
        kernel,
        out_shape=(
            jax.ShapeDtypeStruct((2, DS, K), F32),
            jax.ShapeDtypeStruct((1, ROWS), F32),
        ),
        in_specs=[pl.BlockSpec(memory_space=pltpu.SMEM), vmem, vmem, vmem, anywhere, anywhere, anywhere],
        out_specs=(vmem, vmem),
        scratch_shapes=[
            pltpu.VMEM((ROWS, D), BF16),
            pltpu.VMEM((LISTS, D), BF16),
            pltpu.VMEM((M, DS, K), F32),
            pltpu.VMEM((STEPS, 2 * CW, 2 * K), BF16),
            pltpu.VMEM((SLOTS, ROWS), BF16),
            pltpu.VMEM((1, ROWS), F32),
            pltpu.VMEM((NL * 8, 128), F32),
            pltpu.VMEM((NL * 8, 128), F32),
            pltpu.VMEM((NL, 4, 8, 128), F32),
            pltpu.VMEM((SLOTS, LISTS), BF16),
            pltpu.VMEM((STEPS, SLOTS, CW), BF16),
            pltpu.VMEM((STEPS, SLOTS, CW), BF16),
            pltpu.VMEM((2, SLOTS, CW), F32),
            pltpu.VMEM((2, SLOTS, CW), F32),
            pltpu.VMEM((2, SLOTS, 2 * K), BF16),
            pltpu.VMEM((SLOTS, CW), F32),
            pltpu.VMEM((STEPS, 2, DS, K), F32),
            pltpu.VMEM((STEPS, 2, DS, K), F32),
            pltpu.VMEM((NZ, 4, 1, 128), F32),
            pltpu.VMEM((NZ, 4, 1, 128), F32),
            pltpu.VMEM((4, 1, 128), F32),
            pltpu.VMEM((NL, 1, 128), F32),
            pltpu.VMEM((NL, 8, 128), F32),
            pltpu.VMEM((NL, 8, 128), F32),
            pltpu.VMEM((8, 128), F32),
            pltpu.VMEM((NL, 8, 128), F32),
            pltpu.VMEM((NL * 8, 128), F32),
            pltpu.VMEM((NL * 8, 128), F32),
            dma((3,)),
            dma((2,)),
            dma((STEPS,)),
            dma((STEPS,)),
            dma((STEPS, 2)),
            dma((STEPS, 2)),
            dma((2,)),
            dma((2,)),
            dma((2,)),
            dma((2,)),
            dma((2,)),
        ],
        compiler_params=pltpu.CompilerParams(
            collective_id=0, has_side_effects=True, vmem_limit_bytes=56 * 2**20
        ),
    )(
        valid_rows,
        list_owner.T,
        list_slot.reshape(1, -1),
        pq_codes.T,
        memory_rows,
        centroids,
        codebook.transpose(0, 2, 1),
    )
    return newcb.transpose(0, 2, 1), err.reshape(-1)


def solution(mesh):
    in_specs = (
        P(("list", "rep"), None),
        P(("list", "rep"), None),
        P(("list", "rep")),
        P(("list", "rep"), None),
        P(("list", "rep")),
        P("list", None),
        P(),
    )
    out_specs = (P("rep", None, None), P(("list", "rep")))
    return jax.shard_map(body, mesh=mesh, in_specs=in_specs, out_specs=out_specs, check_vma=False)
```

```python
import functools

import jax
import jax.numpy as jnp
from jax import lax
from jax.experimental import pallas as pl
from jax.experimental.pallas import tpu as pltpu
from jax.sharding import PartitionSpec as P

prior_weight = 4.0

D = 1024
M = 16
K = 256
DS = 64
ROWS = 256
LISTS = 2048
CAP = 32
NL = 32
NZ = 8
SLOTS = NL * CAP
CW = 128
STEPS = D // CW

F32 = jnp.float32
BF16 = jnp.bfloat16
MESH = pl.DeviceIdType.MESH


def iota(shape, axis):
    return lax.broadcasted_iota(jnp.int32, shape, axis)


def dot(a, b, ca, cb):
    return lax.dot_general(a, b, (((ca,), (cb,)), ((), ())), preferred_element_type=F32)


def onehot(mask):
    return jnp.where(mask, 1.0, 0.0).astype(BF16)


def kernel(
    valid,
    owner,
    slot,
    codes,
    rows_hbm,
    cent_hbm,
    cb_hbm,
    newcb,
    err_out,
    rows,
    cents,
    cb,
    cbd,
    place,
    pos_ref,
    mt_send,
    mt_recv,
    meta,
    pick,
    send,
    recv,
    cent,
    recon,
    ohc,
    err,
    zin,
    zout,
    sib_send,
    sib_recv,
    held,
    cz_send,
    cz_recv,
    cx_send,
    cx_recv,
    hand_send,
    hand_recv,
    rs_send,
    rs_recv,
    ag_send,
    ag_recv,
    et_send,
    et_recv,
    local_sem,
    meta_sem,
    data_ss,
    data_rs,
    z_sem,
    sib_ss,
    sib_rs,
    cz_sem,
    cx_sem,
    hand_sem,
    rs_sem,
    ag_sem,
    et_sem,
):
    me = lax.axis_index("list")
    z = lax.axis_index("rep")

    load_rows = pltpu.make_async_copy(rows_hbm, rows, local_sem.at[0])
    load_cb = pltpu.make_async_copy(cb_hbm, cb, local_sem.at[1])
    load_cents = pltpu.make_async_copy(cent_hbm, cents, local_sem.at[2])
    load_rows.start()
    load_cb.start()
    load_cents.start()

    barrier = pltpu.get_barrier_semaphore()

    def greet(k, c):
        pl.semaphore_signal(
            barrier, inc=1, device_id=(lax.rem(me + k, NL), z), device_id_type=MESH
        )
        return c

    def greet_z(k, c):
        pl.semaphore_signal(
            barrier, inc=1, device_id=(me, lax.rem(z + k, NZ)), device_id_type=MESH
        )
        return c

    def greet_planes(k, c):
        for step in (1, NZ - 1):
            pl.semaphore_signal(
                barrier,
                inc=1,
                device_id=(lax.rem(me + k, NL), lax.rem(z + step, NZ)),
                device_id_type=MESH,
            )
        return c

    lax.fori_loop(1, NL, greet, 0)
    lax.fori_loop(1, NZ, greet_z, 0)
    lax.fori_loop(1, NL, greet_planes, 0)

    def peer(k):
        return lax.rem(me + k, NL)

    def copy_to(src, dst, ssem, rsem, who, plane):
        return pltpu.make_async_remote_copy(
            src_ref=src,
            dst_ref=dst,
            send_sem=ssem,
            recv_sem=rsem,
            device_id=(who, plane),
            device_id_type=MESH,
        )

    def pair_at(u, h):
        return lax.rem(z + (3 - u if h else 4 + u), NZ)

    def column(u, h):
        return pl.multiple_of(pair_at(u, h) * CW, CW)

    live = iota((1, ROWS), 1) < valid[0]
    own = jnp.where(live, owner[...], NL)
    named = iota((NL, ROWS), 0) == own
    named_f = jnp.where(named, 1.0, 0.0)
    earlier = onehot(iota((ROWS, ROWS), 0) < iota((ROWS, ROWS), 1))
    before = dot(named_f.astype(BF16), earlier, 1, 0)
    rank = jnp.sum(before * named_f, axis=0, keepdims=True)
    pos = jnp.where(live, own.astype(F32) * CAP + rank, -1.0)
    pos_ref[...] = pos

    def quarter(q):
        i = iota((ROWS, ROWS), 0)
        return ((i // 8) * CAP + q * 8 + i % 8).astype(F32)

    codes_f = jnp.where(live, (codes[...] + 1).astype(F32), 0.0)
    low = (slot[...] % 256).astype(F32)
    high = (slot[...] // 256 + 1).astype(F32)
    which = iota((16, ROWS), 0)
    tail = jnp.where(which == 0, low, jnp.where(which == 1, high, 0.0))
    tail = jnp.where(live, tail, 0.0)
    meta_t = jnp.concatenate([codes_f, tail], axis=0).astype(BF16)
    blank = jnp.zeros((32, ROWS), BF16)
    packed = jnp.zeros((ROWS, 128), F32)
    for q in range(4):
        shifted = jnp.concatenate([meta_t if i == q else blank for i in range(4)], axis=0)
        packed += dot(onehot(quarter(q) == pos), shifted, 1, 1)
    mt_send[...] = packed
    for b in range(4):
        place[pl.ds(b * 256, 256), :] = onehot((iota((256, ROWS), 0) + b * 256).astype(F32) == pos)

    err[...] = jnp.zeros((SLOTS, CW), F32)

    load_rows.wait()

    def bucket(v):
        first = 2 * v
        both = jnp.concatenate(
            [rows[:, pl.ds(column(v, 0), CW)], rows[:, pl.ds(column(v, 1), CW)]], axis=1
        )
        for b in range(4):
            part = dot(place[pl.ds(b * 256, 256), :], both, 1, 0).astype(BF16)
            send[first, pl.ds(b * 256, 256), :] = part[:, :CW]
            send[first + 1, pl.ds(b * 256, 256), :] = part[:, CW:]

    bucket(0)
    pl.semaphore_wait(barrier, 3 * (NL - 1) + NZ - 1)

    def tile8(j):
        return pl.ds(pl.multiple_of(j * 8, 8), 8)

    def tile32(j):
        return pl.ds(pl.multiple_of(j * CAP, CAP), CAP)

    def start(v, h):
        c = 2 * v + h
        for k in range(1, NL):
            j = peer(k)
            copy_to(
                send.at[c, tile32(j)], recv.at[c, tile32(me)], data_ss.at[c], data_rs.at[c], j, z
            ).start()
        recv[c, tile32(me), :] = send[c, tile32(me), :]

    def send_meta(k, c):
        j = peer(k)
        copy_to(mt_send.at[tile8(j)], mt_recv.at[tile8(me)], meta_sem.at[0], meta_sem.at[1], j, z).start()
        return c

    lax.fori_loop(1, NL, send_meta, 0)
    mt_recv[tile8(me), :] = mt_send[tile8(me), :]


    start(0, 0)
    start(0, 1)

    eye = onehot(iota((ROWS, ROWS), 0) == iota((ROWS, ROWS), 1))
    natural = dot(eye, meta_t, 1, 1)
    code_lane = (iota((ROWS, K), 1) + 1).astype(F32)
    code_lane2 = (iota((1024, K), 1) + 1).astype(F32)
    ones = jnp.ones((16, ROWS), BF16)
    for m in range(M):
        tally = dot(ones, onehot(natural[:, m : m + 1] == code_lane), 1, 0)
        for h in range(2):
            cz_send[m // 2, (m % 2) * 2 + h] = tally[0:1, h * 128 : (h + 1) * 128]

    def send_cz(k, c):
        other = lax.rem(z + k, NZ)
        copy_to(cz_send.at[other], cz_recv.at[z], cz_sem.at[0], cz_sem.at[1], me, other).start()
        return c

    lax.fori_loop(1, NZ, send_cz, 0)
    cz_recv[z] = cz_send[z]

    load_cb.wait()
    for p in range(STEPS):
        none = jnp.zeros((DS, K), F32)
        top = jnp.concatenate([cb[2 * p], none], axis=1)
        bottom = jnp.concatenate([none, cb[2 * p + 1]], axis=1)
        block = jnp.concatenate([top, bottom], axis=0)
        coarse = block.astype(BF16)
        cbd[p, 0:CW, :] = coarse
        cbd[p, CW : 2 * CW, :] = (block - coarse.astype(F32)).astype(BF16)

    copy_to(
        mt_send.at[pl.ds(0, 248)], mt_recv.at[pl.ds(0, 248)], meta_sem.at[0], meta_sem.at[1], me, z
    ).wait_recv()
    got = mt_recv[...]
    for q in range(4):
        turned = got if q == 0 else pltpu.roll(got, 128 - 32 * q, 1)
        meta[:, q] = turned.reshape(NL, 8, 128)

    def meta_rows(b):
        return meta[pl.ds(b * 32, 32)].reshape(1024, 128)

    def build_pick(b, c):
        m = meta_rows(b)
        wanted = m[:, 17:18] * 256.0 + m[:, 16:17] - 256.0
        for t in range(4):
            lanes = (iota((1024, 512), 1) + t * 512).astype(F32)
            pick[pl.ds(b * 1024, 1024), t * 512 : (t + 1) * 512] = onehot(wanted == lanes)
        return c

    lax.fori_loop(0, 1, build_pick, 0)
    load_cents.wait()

    core = lax.rem(me, 2)
    sibling = me + 1 - 2 * core

    def share(s, mine, theirs):
        zout[s] = mine
        sib_send[s] = theirs
        copy_to(sib_send.at[s], sib_recv.at[s], sib_ss.at[s], sib_rs.at[s], sibling, z).start()

    def forward(u, h):
        s = 2 * u + h
        copy_to(sib_send.at[s], sib_recv.at[s], sib_ss.at[s], sib_rs.at[s], sibling, z).wait_recv()
        zout[s] = zout[s] + sib_recv[s]
        copy_to(zout.at[s], zin.at[s], z_sem.at[0], z_sem.at[1], me, pair_at(u, h)).start()

    def pass_counts():
        copy_to(
            cz_send.at[pl.ds(0, NZ - 1)], cz_recv.at[pl.ds(0, NZ - 1)], cz_sem.at[0], cz_sem.at[1], me, z
        ).wait_recv()
        cx_send[...] = jnp.sum(cz_recv[...], axis=0)

        def send_cx(k, c):
            j = peer(k)
            piece = (j // 16) * 2 + lax.rem(j, 2)
            copy_to(cx_send.at[piece], cx_recv.at[me], cx_sem.at[0], cx_sem.at[1], j, z).start()
            return c

        lax.fori_loop(1, NL, send_cx, 0)
        cx_recv[me] = cx_send[(me // 16) * 2 + lax.rem(me, 2)]

    def piece_of(sums, i):
        a, d, h = i // 16, (i // 2) % 8, i % 2
        return sums[a][d * 8 : (d + 1) * 8, h * 128 : (h + 1) * 128]

    def send_hand(k, c):
        j = peer(k)
        copy_to(
            hand_send.at[j], hand_recv.at[me], hand_sem.at[0], hand_sem.at[1], j, pair_at(3, 0)
        ).start()
        return c

    def two_steps(u, carry):
        @pl.when(u < 3)
        def _():
            bucket(u + 1)
            start(u + 1, 0)

        table = jnp.concatenate(
            [cents[:, pl.ds(column(u, 0), CW)], cents[:, pl.ds(column(u, 1), CW)]], axis=1
        )

        def ahead(b, c):
            r = pl.ds(b * 1024, 1024)
            centre = dot(pick[r, :], table, 1, 0)
            m = meta_rows(b)
            for h in range(2):
                p = pair_at(u, h)
                cent[h, r, :] = centre[:, h * CW : (h + 1) * CW]
                turned = pltpu.roll(m, lax.rem(128 - 2 * p, 128), 1)
                hot = jnp.concatenate(
                    [onehot(turned[:, 0:1] == code_lane2), onehot(turned[:, 1:2] == code_lane2)], axis=1
                )
                ohc[h, r, :] = hot
                value = dot(hot, cbd[p], 1, 1)
                recon[h, r, :] = value[:, :CW] + value[:, CW:]
            return c

        lax.fori_loop(0, 1, ahead, 0)

        @pl.when(u > 0)
        def _():
            forward(u - 1, 0)
            forward(u - 1, 1)

        pl.when(u == 1)(pass_counts)

        for h in range(2):
            s = 2 * u + h
            copy_to(
                send.at[s, pl.ds(0, SLOTS - CAP)],
                recv.at[s, pl.ds(0, SLOTS - CAP)],
                data_ss.at[s],
                data_rs.at[s],
                me,
                z,
            ).wait_recv()

            total = jnp.zeros((CW, 2 * K), F32)
            for b in range(4):
                r = pl.ds(b * 256, 256)
                residual = recv[s, r, :].astype(F32) - cent[h, r, :]
                gap = residual - recon[h, r, :]
                err[r, :] += gap * gap
                total += dot(residual.astype(BF16), ohc[h, r, :], 0, 0)
            first, second = total[:DS, :K], total[DS:, K:]
            mine = jnp.where(core == 0, first, second)
            theirs = jnp.where(core == 0, second, first)

            @pl.when(u < 3)
            def _():
                share(s, mine, theirs)
                if h == 0:
                    start(u + 1, 1)

            @pl.when(u == 3)
            def _():
                if h == 1:
                    held[0] = first
                    held[1] = second
                else:
                    for i in range(NL):
                        hand_send[i] = piece_of((first, second), i)
                    lax.fori_loop(0, NL, send_hand, 0)

        return carry

    lax.fori_loop(0, STEPS // 2, two_steps, 0)

    z_all = copy_to(
        zout, zin, z_sem.at[0], z_sem.at[1], me, z
    )
    z_all.wait_recv()
    others = jnp.sum(zin[...], axis=0)
    plane_sum = [held[a] + jnp.where(core == a, others, 0.0) for a in range(2)]

    for i in range(NL):
        rs_send[i] = piece_of(plane_sum, i)

    def send_rs(k, c):
        j = peer(k)
        copy_to(rs_send.at[j], rs_recv.at[me], rs_sem.at[0], rs_sem.at[1], j, z).start()
        return c

    lax.fori_loop(1, NL, send_rs, 0)
    rs_recv[me] = rs_send[me]

    summed = (jnp.sum(err[...], axis=1, keepdims=True) * (1.0 / D)).reshape(NL, 4, 8, 1)
    lane = iota((NL, 8, 128), 2)
    tiles = jnp.zeros((NL, 8, 128), F32)
    for q in range(4):
        tiles = jnp.where(lane // 32 == q, summed[:, q], tiles)
    tiles = jnp.where((lane % 32) // 4 == iota((NL, 8, 128), 1), tiles, 0.0)
    et_send[...] = jnp.sum(tiles, axis=1, keepdims=True)

    def send_et(k, c):
        j = peer(k)
        copy_to(et_send.at[j], et_recv.at[me], et_sem.at[0], et_sem.at[1], j, z).start()
        return c

    lax.fori_loop(1, NL, send_et, 0)
    et_recv[me] = et_send[me]

    def wait_all(src, dst, sem):
        whole = copy_to(src, dst, sem.at[0], sem.at[1], me, z)
        return whole

    first31 = pl.ds(0, NL - 1)
    cx_all = wait_all(cx_recv.at[first31], cx_recv.at[first31], cx_sem)
    rs_all = wait_all(rs_send.at[first31], rs_recv.at[first31], rs_sem)
    hand_all = wait_all(hand_send, hand_recv, hand_sem)
    ag_all = wait_all(ag_recv.at[first31], ag_recv.at[first31], ag_sem)
    et_all = wait_all(et_send.at[first31], et_recv.at[first31], et_sem)

    cx_all.wait_recv()
    count = jnp.sum(cx_recv[...], axis=0)
    rs_all.wait_recv()
    hand_all.wait_recv()
    total = jnp.sum(rs_recv[...] + hand_recv[...], axis=0)
    old = cb[
        2 * z + me // 16,
        pl.ds(pl.multiple_of(lax.rem(me // 2, 8) * 8, 8), 8),
        pl.ds(pl.multiple_of(lax.rem(me, 2) * 128, 128), 128),
    ]
    ag_send[...] = (total + prior_weight * old) / (count + prior_weight)

    def send_ag(k, c):
        j = peer(k)
        copy_to(ag_send, ag_recv.at[me], ag_sem.at[0], ag_sem.at[1], j, z).start()
        return c

    lax.fori_loop(1, NL, send_ag, 0)
    ag_recv[me] = ag_send[...]

    et_all.wait_recv()
    rest = et_recv[...].reshape(NL, 128)
    holder = pos_ref[...]
    owner_of = jnp.floor(holder * (1.0 / CAP))
    at = onehot(iota((128, ROWS), 0).astype(F32) == (holder - owner_of * CAP) * 4.0)
    picked = jnp.zeros((NL, ROWS), F32)
    for _ in range(3):
        part = rest.astype(BF16)
        rest = rest - part.astype(F32)
        picked += dot(part, at, 1, 0)
    belongs = iota((NL, ROWS), 0).astype(F32) == owner_of
    err_out[...] = jnp.sum(jnp.where(belongs, picked, 0.0), axis=0, keepdims=True)

    ag_all.wait_recv()
    for a in range(2):
        for d in range(8):
            for h in range(2):
                newcb[a, d * 8 : (d + 1) * 8, h * 128 : (h + 1) * 128] = ag_recv[a * 16 + d * 2 + h]

    copy_to(
        mt_send.at[pl.ds(0, 248)], mt_recv.at[pl.ds(0, 248)], meta_sem.at[0], meta_sem.at[1], me, z
    ).wait_send()
    copy_to(
        cz_send.at[pl.ds(0, NZ - 1)], cz_recv.at[pl.ds(0, NZ - 1)], cz_sem.at[0], cz_sem.at[1], me, z
    ).wait_send()

    def drain(s, c):
        copy_to(
            send.at[s, pl.ds(0, SLOTS - CAP)],
            recv.at[s, pl.ds(0, SLOTS - CAP)],
            data_ss.at[s],
            data_rs.at[s],
            me,
            z,
        ).wait_send()
        return c

    lax.fori_loop(0, STEPS, drain, 0)

    z_all.wait_send()

    def drain_share(i, c):
        copy_to(sib_send.at[i], sib_recv.at[i], sib_ss.at[i], sib_rs.at[i], sibling, z).wait_send()
        return c

    lax.fori_loop(0, STEPS - 2, drain_share, 0)
    cx_all.wait_send()
    hand_all.wait_send()
    rs_all.wait_send()
    et_all.wait_send()
    ag_all.wait_send()


def hand_over(newcb_in, err_in, newcb_out, err_out):
    newcb_out[...] = newcb_in[...]
    err_out[...] = err_in[...]


def body(memory_rows, list_owner, list_slot, pq_codes, valid_rows, centroids, codebook):
    vmem = pl.BlockSpec(memory_space=pltpu.VMEM)
    anywhere = pl.BlockSpec(memory_space=pl.ANY)
    dma = pltpu.SemaphoreType.DMA
    newcb, err = pl.pallas_call(
        kernel,
        out_shape=(
            jax.ShapeDtypeStruct((2, DS, K), F32),
            jax.ShapeDtypeStruct((1, ROWS), F32),
        ),
        in_specs=[pl.BlockSpec(memory_space=pltpu.SMEM), vmem, vmem, vmem, anywhere, anywhere, anywhere],
        out_specs=(vmem, vmem),
        scratch_shapes=[
            pltpu.VMEM((ROWS, D), BF16),
            pltpu.VMEM((LISTS, D), BF16),
            pltpu.VMEM((M, DS, K), F32),
            pltpu.VMEM((STEPS, 2 * CW, 2 * K), BF16),
            pltpu.VMEM((SLOTS, ROWS), BF16),
            pltpu.VMEM((1, ROWS), F32),
            pltpu.VMEM((NL * 8, 128), F32),
            pltpu.VMEM((NL * 8, 128), F32),
            pltpu.VMEM((NL, 4, 8, 128), F32),
            pltpu.VMEM((SLOTS, LISTS), BF16),
            pltpu.VMEM((STEPS, SLOTS, CW), BF16),
            pltpu.VMEM((STEPS, SLOTS, CW), BF16),
            pltpu.VMEM((2, SLOTS, CW), F32),
            pltpu.VMEM((2, SLOTS, CW), F32),
            pltpu.VMEM((2, SLOTS, 2 * K), BF16),
            pltpu.VMEM((SLOTS, CW), F32),
            pltpu.VMEM((STEPS - 2, DS, K), F32),
            pltpu.VMEM((STEPS - 2, DS, K), F32),
            pltpu.VMEM((STEPS - 2, DS, K), F32),
            pltpu.VMEM((STEPS - 2, DS, K), F32),
            pltpu.VMEM((2, DS, K), F32),
            pltpu.VMEM((NZ, 4, 1, 128), F32),
            pltpu.VMEM((NZ, 4, 1, 128), F32),
            pltpu.VMEM((4, 1, 128), F32),
            pltpu.VMEM((NL, 1, 128), F32),
            pltpu.VMEM((NL, 8, 128), F32),
            pltpu.VMEM((NL, 8, 128), F32),
            pltpu.VMEM((NL, 8, 128), F32),
            pltpu.VMEM((NL, 8, 128), F32),
            pltpu.VMEM((8, 128), F32),
            pltpu.VMEM((NL, 8, 128), F32),
            pltpu.VMEM((NL, 1, 128), F32),
            pltpu.VMEM((NL, 1, 128), F32),
            dma((3,)),
            dma((2,)),
            dma((STEPS,)),
            dma((STEPS,)),
            dma((2,)),
            dma((STEPS - 2,)),
            dma((STEPS - 2,)),
            dma((2,)),
            dma((2,)),
            dma((2,)),
            dma((2,)),
            dma((2,)),
            dma((2,)),
        ],
        compiler_params=pltpu.CompilerParams(
            collective_id=0, has_side_effects=True, vmem_limit_bytes=56 * 2**20
        ),
    )(
        valid_rows,
        list_owner.T,
        list_slot.reshape(1, -1),
        pq_codes.T,
        memory_rows,
        centroids,
        codebook.transpose(0, 2, 1),
    )
    newcb, err = pl.pallas_call(
        hand_over,
        out_shape=(
            jax.ShapeDtypeStruct((2, DS, K), F32),
            jax.ShapeDtypeStruct((1, ROWS), F32),
        ),
        in_specs=[vmem, vmem],
        out_specs=(vmem, vmem),
    )(newcb, err)
    return newcb.transpose(0, 2, 1), err.reshape(-1)


def solution(mesh):
    in_specs = (
        P(("list", "rep"), None),
        P(("list", "rep"), None),
        P(("list", "rep")),
        P(("list", "rep"), None),
        P(("list", "rep")),
        P("list", None),
        P(),
    )
    out_specs = (P("rep", None, None), P(("list", "rep")))
    return jax.shard_map(body, mesh=mesh, in_specs=in_specs, out_specs=out_specs, check_vma=False)
```

```python
import functools

import jax
import jax.numpy as jnp
from jax import lax
from jax.experimental import pallas as pl
from jax.experimental.pallas import tpu as pltpu
from jax.sharding import PartitionSpec as P

prior_weight = 4.0

D = 1024
M = 16
K = 256
DS = 64
ROWS = 256
LISTS = 2048
CAP = 32
NL = 32
NZ = 8
SLOTS = NL * CAP
CW = 128
STEPS = D // CW

F32 = jnp.float32
BF16 = jnp.bfloat16
MESH = pl.DeviceIdType.MESH


def iota(shape, axis):
    return lax.broadcasted_iota(jnp.int32, shape, axis)


def dot(a, b, ca, cb):
    return lax.dot_general(a, b, (((ca,), (cb,)), ((), ())), preferred_element_type=F32)


def onehot(mask):
    return jnp.where(mask, 1.0, 0.0).astype(BF16)


def kernel(
    valid,
    owner,
    slot,
    codes,
    rows_hbm,
    cent_hbm,
    cb_hbm,
    newcb,
    err_out,
    rows,
    cents,
    cb,
    cbd,
    place,
    pos_ref,
    mt_send,
    mt_recv,
    meta,
    pick,
    send,
    recv,
    cent,
    recon,
    ohc,
    err,
    zin,
    zout,
    sib_send,
    sib_recv,
    held,
    cz_send,
    cz_recv,
    cx_send,
    cx_recv,
    hand_send,
    hand_recv,
    rs_send,
    rs_recv,
    ag_send,
    et_send,
    et_recv,
    local_sem,
    meta_sem,
    data_ss,
    data_rs,
    z_sem,
    sib_ss,
    sib_rs,
    cz_sem,
    cx_sem,
    hand_sem,
    rs_sem,
    ag_sem,
    et_sem,
):
    me = lax.axis_index("list")
    z = lax.axis_index("rep")

    load_rows = pltpu.make_async_copy(rows_hbm, rows, local_sem.at[0])
    load_cb = pltpu.make_async_copy(cb_hbm, cb, local_sem.at[1])
    load_cents = pltpu.make_async_copy(cent_hbm, cents, local_sem.at[2])
    load_rows.start()
    load_cb.start()
    load_cents.start()

    barrier = pltpu.get_barrier_semaphore()

    def greet(k, c):
        pl.semaphore_signal(
            barrier, inc=1, device_id=(lax.rem(me + k, NL), z), device_id_type=MESH
        )
        return c

    def greet_z(k, c):
        pl.semaphore_signal(
            barrier, inc=1, device_id=(me, lax.rem(z + k, NZ)), device_id_type=MESH
        )
        return c

    def greet_planes(k, c):
        for step in (1, NZ - 1):
            pl.semaphore_signal(
                barrier,
                inc=1,
                device_id=(lax.rem(me + k, NL), lax.rem(z + step, NZ)),
                device_id_type=MESH,
            )
        return c

    lax.fori_loop(1, NL, greet, 0)
    lax.fori_loop(1, NZ, greet_z, 0)
    lax.fori_loop(1, NL, greet_planes, 0)

    def peer(k):
        return lax.rem(me + k, NL)

    def ring(steps):
        return min(steps, 4 - steps)

    offsets = [(dx, dy, dc) for dx in range(4) for dy in range(4) for dc in range(2)]
    offsets.sort(key=lambda o: -(ring(o[0]) + ring(o[1])))

    def far_first():
        x, y, c = me // 8, lax.rem(me // 2, 4), lax.rem(me, 2)
        for dx, dy, dc in offsets[:-2]:
            yield (lax.rem(x + dx, 4) * 4 + lax.rem(y + dy, 4)) * 2 + lax.rem(c + dc, 2)
        yield me + 1 - 2 * c

    def copy_to(src, dst, ssem, rsem, who, plane):
        return pltpu.make_async_remote_copy(
            src_ref=src,
            dst_ref=dst,
            send_sem=ssem,
            recv_sem=rsem,
            device_id=(who, plane),
            device_id_type=MESH,
        )

    def pair_at(u, h):
        return lax.rem(z + (3 - u if h else 4 + u), NZ)

    def column(u, h):
        return pl.multiple_of(pair_at(u, h) * CW, CW)

    live = iota((1, ROWS), 1) < valid[0]
    own = jnp.where(live, owner[...], NL)
    named = iota((NL, ROWS), 0) == own
    named_f = jnp.where(named, 1.0, 0.0)
    earlier = onehot(iota((ROWS, ROWS), 0) < iota((ROWS, ROWS), 1))
    before = dot(named_f.astype(BF16), earlier, 1, 0)
    rank = jnp.sum(before * named_f, axis=0, keepdims=True)
    pos = jnp.where(live, own.astype(F32) * CAP + rank, -1.0)
    pos_ref[...] = pos

    def quarter(q):
        i = iota((ROWS, ROWS), 0)
        return ((i // 8) * CAP + q * 8 + i % 8).astype(F32)

    codes_f = jnp.where(live, (codes[...] + 1).astype(F32), 0.0)
    low = (slot[...] % 256).astype(F32)
    high = (slot[...] // 256 + 1).astype(F32)
    which = iota((16, ROWS), 0)
    tail = jnp.where(which == 0, low, jnp.where(which == 1, high, 0.0))
    tail = jnp.where(live, tail, 0.0)
    meta_t = jnp.concatenate([codes_f, tail], axis=0).astype(BF16)
    blank = jnp.zeros((32, ROWS), BF16)
    packed = jnp.zeros((ROWS, 128), F32)
    for q in range(4):
        shifted = jnp.concatenate([meta_t if i == q else blank for i in range(4)], axis=0)
        packed += dot(onehot(quarter(q) == pos), shifted, 1, 1)
    mt_send[...] = packed
    for b in range(4):
        place[pl.ds(b * 256, 256), :] = onehot((iota((256, ROWS), 0) + b * 256).astype(F32) == pos)

    err[...] = jnp.zeros((SLOTS, CW), F32)

    load_rows.wait()

    def bucket(v):
        first = 2 * v
        both = jnp.concatenate(
            [rows[:, pl.ds(column(v, 0), CW)], rows[:, pl.ds(column(v, 1), CW)]], axis=1
        )
        for b in range(4):
            part = dot(place[pl.ds(b * 256, 256), :], both, 1, 0).astype(BF16)
            send[first, pl.ds(b * 256, 256), :] = part[:, :CW]
            send[first + 1, pl.ds(b * 256, 256), :] = part[:, CW:]

    bucket(0)
    pl.semaphore_wait(barrier, 3 * (NL - 1) + NZ - 1)

    def tile8(j):
        return pl.ds(pl.multiple_of(j * 8, 8), 8)

    def tile32(j):
        return pl.ds(pl.multiple_of(j * CAP, CAP), CAP)

    def start(v, h):
        c = 2 * v + h
        for k in range(1, NL):
            j = peer(k)
            copy_to(
                send.at[c, tile32(j)], recv.at[c, tile32(me)], data_ss.at[c], data_rs.at[c], j, z
            ).start()
        recv[c, tile32(me), :] = send[c, tile32(me), :]

    def send_meta(k, c):
        j = peer(k)
        copy_to(mt_send.at[tile8(j)], mt_recv.at[tile8(me)], meta_sem.at[0], meta_sem.at[1], j, z).start()
        return c

    lax.fori_loop(1, NL, send_meta, 0)
    mt_recv[tile8(me), :] = mt_send[tile8(me), :]


    start(0, 0)
    start(0, 1)

    eye = onehot(iota((ROWS, ROWS), 0) == iota((ROWS, ROWS), 1))
    natural = dot(eye, meta_t, 1, 1)
    code_lane = (iota((ROWS, K), 1) + 1).astype(F32)
    code_lane2 = (iota((1024, K), 1) + 1).astype(F32)
    ones = jnp.ones((16, ROWS), BF16)
    for m in range(M):
        tally = dot(ones, onehot(natural[:, m : m + 1] == code_lane), 1, 0)
        for h in range(2):
            cz_send[m // 2, (m % 2) * 2 + h] = tally[0:1, h * 128 : (h + 1) * 128]

    def send_cz(k, c):
        other = lax.rem(z + k, NZ)
        copy_to(cz_send.at[other], cz_recv.at[z], cz_sem.at[0], cz_sem.at[1], me, other).start()
        return c

    lax.fori_loop(1, NZ, send_cz, 0)
    cz_recv[z] = cz_send[z]

    load_cb.wait()
    for p in range(STEPS):
        none = jnp.zeros((DS, K), F32)
        top = jnp.concatenate([cb[2 * p], none], axis=1)
        bottom = jnp.concatenate([none, cb[2 * p + 1]], axis=1)
        block = jnp.concatenate([top, bottom], axis=0)
        coarse = block.astype(BF16)
        cbd[p, 0:CW, :] = coarse
        cbd[p, CW : 2 * CW, :] = (block - coarse.astype(F32)).astype(BF16)

    copy_to(
        mt_send.at[pl.ds(0, 248)], mt_recv.at[pl.ds(0, 248)], meta_sem.at[0], meta_sem.at[1], me, z
    ).wait_recv()
    got = mt_recv[...]
    for q in range(4):
        turned = got if q == 0 else pltpu.roll(got, 128 - 32 * q, 1)
        meta[:, q] = turned.reshape(NL, 8, 128)

    def meta_rows(b):
        return meta[pl.ds(b * 32, 32)].reshape(1024, 128)

    def build_pick(b, c):
        m = meta_rows(b)
        wanted = m[:, 17:18] * 256.0 + m[:, 16:17] - 256.0
        for t in range(4):
            lanes = (iota((1024, 512), 1) + t * 512).astype(F32)
            pick[pl.ds(b * 1024, 1024), t * 512 : (t + 1) * 512] = onehot(wanted == lanes)
        return c

    lax.fori_loop(0, 1, build_pick, 0)
    load_cents.wait()

    core = lax.rem(me, 2)
    sibling = me + 1 - 2 * core

    def share(s, mine, theirs):
        zout[s] = mine
        sib_send[s] = theirs
        copy_to(sib_send.at[s], sib_recv.at[s], sib_ss.at[s], sib_rs.at[s], sibling, z).start()

    def forward(u, h):
        s = 2 * u + h
        copy_to(sib_send.at[s], sib_recv.at[s], sib_ss.at[s], sib_rs.at[s], sibling, z).wait_recv()
        zout[s] = zout[s] + sib_recv[s]
        copy_to(zout.at[s], zin.at[s], z_sem.at[0], z_sem.at[1], me, pair_at(u, h)).start()

    def pass_counts():
        copy_to(
            cz_send.at[pl.ds(0, NZ - 1)], cz_recv.at[pl.ds(0, NZ - 1)], cz_sem.at[0], cz_sem.at[1], me, z
        ).wait_recv()
        cx_send[...] = jnp.sum(cz_recv[...], axis=0)

        def send_cx(k, c):
            j = peer(k)
            piece = (j // 16) * 2 + lax.rem(j, 2)
            copy_to(cx_send.at[piece], cx_recv.at[me], cx_sem.at[0], cx_sem.at[1], j, z).start()
            return c

        lax.fori_loop(1, NL, send_cx, 0)
        cx_recv[me] = cx_send[(me // 16) * 2 + lax.rem(me, 2)]

    def piece_of(sums, i):
        a, d, h = i // 16, (i // 2) % 8, i % 2
        return sums[a][d * 8 : (d + 1) * 8, h * 128 : (h + 1) * 128]

    def send_hand(k, c):
        j = peer(k)
        copy_to(
            hand_send.at[j], hand_recv.at[me], hand_sem.at[0], hand_sem.at[1], j, pair_at(3, 0)
        ).start()
        return c

    def two_steps(u, carry):
        @pl.when(u < 3)
        def _():
            bucket(u + 1)
            start(u + 1, 0)

        table = jnp.concatenate(
            [cents[:, pl.ds(column(u, 0), CW)], cents[:, pl.ds(column(u, 1), CW)]], axis=1
        )

        def ahead(b, c):
            r = pl.ds(b * 1024, 1024)
            centre = dot(pick[r, :], table, 1, 0)
            m = meta_rows(b)
            for h in range(2):
                p = pair_at(u, h)
                cent[h, r, :] = centre[:, h * CW : (h + 1) * CW]
                turned = pltpu.roll(m, lax.rem(128 - 2 * p, 128), 1)
                hot = jnp.concatenate(
                    [onehot(turned[:, 0:1] == code_lane2), onehot(turned[:, 1:2] == code_lane2)], axis=1
                )
                ohc[h, r, :] = hot
                value = dot(hot, cbd[p], 1, 1)
                recon[h, r, :] = value[:, :CW] + value[:, CW:]
            return c

        lax.fori_loop(0, 1, ahead, 0)

        @pl.when(u > 0)
        def _():
            forward(u - 1, 0)
            forward(u - 1, 1)

        pl.when(u == 1)(pass_counts)

        for h in range(2):
            s = 2 * u + h
            copy_to(
                send.at[s, pl.ds(0, SLOTS - CAP)],
                recv.at[s, pl.ds(0, SLOTS - CAP)],
                data_ss.at[s],
                data_rs.at[s],
                me,
                z,
            ).wait_recv()

            total = jnp.zeros((CW, 2 * K), F32)
            for b in range(4):
                r = pl.ds(b * 256, 256)
                residual = recv[s, r, :].astype(F32) - cent[h, r, :]
                gap = residual - recon[h, r, :]
                err[r, :] += gap * gap
                total += dot(residual.astype(BF16), ohc[h, r, :], 0, 0)
            first, second = total[:DS, :K], total[DS:, K:]
            mine = jnp.where(core == 0, first, second)
            theirs = jnp.where(core == 0, second, first)

            @pl.when(u < 3)
            def _():
                share(s, mine, theirs)
                if h == 0:
                    start(u + 1, 1)

            @pl.when(u == 3)
            def _():
                if h == 1:
                    held[0] = first
                    held[1] = second
                else:
                    for i in range(NL):
                        hand_send[i] = piece_of((first, second), i)
                    lax.fori_loop(0, NL, send_hand, 0)

        return carry

    lax.fori_loop(0, STEPS // 2, two_steps, 0)

    z_all = copy_to(
        zout, zin, z_sem.at[0], z_sem.at[1], me, z
    )
    z_all.wait_recv()
    others = jnp.sum(zin[...], axis=0)
    plane_sum = [held[a] + jnp.where(core == a, others, 0.0) for a in range(2)]

    for i in range(NL):
        rs_send[i] = piece_of(plane_sum, i)

    for j in far_first():
        copy_to(rs_send.at[j], rs_recv.at[me], rs_sem.at[0], rs_sem.at[1], j, z).start()
    rs_recv[me] = rs_send[me]

    summed = (jnp.sum(err[...], axis=1, keepdims=True) * (1.0 / D)).reshape(NL, 4, 8, 1)
    lane = iota((NL, 8, 128), 2)
    tiles = jnp.zeros((NL, 8, 128), F32)
    for q in range(4):
        tiles = jnp.where(lane // 32 == q, summed[:, q], tiles)
    tiles = jnp.where((lane % 32) // 4 == iota((NL, 8, 128), 1), tiles, 0.0)
    et_send[...] = jnp.sum(tiles, axis=1, keepdims=True)

    def send_et(k, c):
        j = peer(k)
        copy_to(et_send.at[j], et_recv.at[me], et_sem.at[0], et_sem.at[1], j, z).start()
        return c

    lax.fori_loop(1, NL, send_et, 0)
    et_recv[me] = et_send[me]

    def wait_all(src, dst, sem):
        whole = copy_to(src, dst, sem.at[0], sem.at[1], me, z)
        return whole

    first31 = pl.ds(0, NL - 1)
    cx_all = wait_all(cx_recv.at[first31], cx_recv.at[first31], cx_sem)
    rs_all = wait_all(rs_send.at[first31], rs_recv.at[first31], rs_sem)
    hand_all = wait_all(hand_send, hand_recv, hand_sem)
    ag_all = wait_all(rs_send.at[first31], rs_recv.at[first31], ag_sem)
    et_all = wait_all(et_send.at[first31], et_recv.at[first31], et_sem)

    cx_all.wait_recv()
    count = jnp.sum(cx_recv[...], axis=0)
    rs_all.wait_recv()
    hand_all.wait_recv()
    total = jnp.sum(rs_recv[...] + hand_recv[...], axis=0)

    def place_of(ref, i):
        rows_at = pl.ds(pl.multiple_of(lax.rem(i // 2, 8) * 8, 8), 8)
        return ref.at[i // 16, rows_at, pl.ds(pl.multiple_of(lax.rem(i, 2) * 128, 128), 128)]

    old = cb[
        2 * z + me // 16,
        pl.ds(pl.multiple_of(lax.rem(me // 2, 8) * 8, 8), 8),
        pl.ds(pl.multiple_of(lax.rem(me, 2) * 128, 128), 128),
    ]
    ag_send[...] = (total + prior_weight * old) / (count + prior_weight)

    for j in far_first():
        copy_to(ag_send, place_of(newcb, me), ag_sem.at[0], ag_sem.at[1], j, z).start()
    own_piece = pltpu.make_async_copy(ag_send, place_of(newcb, me), local_sem.at[3])
    own_piece.start()

    et_all.wait_recv()
    rest = et_recv[...].reshape(NL, 128)
    holder = pos_ref[...]
    owner_of = jnp.floor(holder * (1.0 / CAP))
    at = onehot(iota((128, ROWS), 0).astype(F32) == (holder - owner_of * CAP) * 4.0)
    picked = jnp.zeros((NL, ROWS), F32)
    for _ in range(3):
        part = rest.astype(BF16)
        rest = rest - part.astype(F32)
        picked += dot(part, at, 1, 0)
    belongs = iota((NL, ROWS), 0).astype(F32) == owner_of
    err_out[...] = jnp.sum(jnp.where(belongs, picked, 0.0), axis=0, keepdims=True)

    ag_all.wait_recv()
    own_piece.wait()

    copy_to(
        mt_send.at[pl.ds(0, 248)], mt_recv.at[pl.ds(0, 248)], meta_sem.at[0], meta_sem.at[1], me, z
    ).wait_send()
    copy_to(
        cz_send.at[pl.ds(0, NZ - 1)], cz_recv.at[pl.ds(0, NZ - 1)], cz_sem.at[0], cz_sem.at[1], me, z
    ).wait_send()

    def drain(s, c):
        copy_to(
            send.at[s, pl.ds(0, SLOTS - CAP)],
            recv.at[s, pl.ds(0, SLOTS - CAP)],
            data_ss.at[s],
            data_rs.at[s],
            me,
            z,
        ).wait_send()
        return c

    lax.fori_loop(0, STEPS, drain, 0)

    z_all.wait_send()

    def drain_share(i, c):
        copy_to(sib_send.at[i], sib_recv.at[i], sib_ss.at[i], sib_rs.at[i], sibling, z).wait_send()
        return c

    lax.fori_loop(0, STEPS - 2, drain_share, 0)
    cx_all.wait_send()
    hand_all.wait_send()
    rs_all.wait_send()
    et_all.wait_send()
    ag_all.wait_send()


def hand_over(newcb_in, err_in, newcb_out, err_out):
    newcb_out[...] = newcb_in[...]
    err_out[...] = err_in[...]


def body(memory_rows, list_owner, list_slot, pq_codes, valid_rows, centroids, codebook):
    vmem = pl.BlockSpec(memory_space=pltpu.VMEM)
    anywhere = pl.BlockSpec(memory_space=pl.ANY)
    dma = pltpu.SemaphoreType.DMA
    newcb, err = pl.pallas_call(
        kernel,
        out_shape=(
            jax.ShapeDtypeStruct((2, DS, K), F32),
            jax.ShapeDtypeStruct((1, ROWS), F32),
        ),
        in_specs=[pl.BlockSpec(memory_space=pltpu.SMEM), vmem, vmem, vmem, anywhere, anywhere, anywhere],
        out_specs=(anywhere, vmem),
        scratch_shapes=[
            pltpu.VMEM((ROWS, D), BF16),
            pltpu.VMEM((LISTS, D), BF16),
            pltpu.VMEM((M, DS, K), F32),
            pltpu.VMEM((STEPS, 2 * CW, 2 * K), BF16),
            pltpu.VMEM((SLOTS, ROWS), BF16),
            pltpu.VMEM((1, ROWS), F32),
            pltpu.VMEM((NL * 8, 128), F32),
            pltpu.VMEM((NL * 8, 128), F32),
            pltpu.VMEM((NL, 4, 8, 128), F32),
            pltpu.VMEM((SLOTS, LISTS), BF16),
            pltpu.VMEM((STEPS, SLOTS, CW), BF16),
            pltpu.VMEM((STEPS, SLOTS, CW), BF16),
            pltpu.VMEM((2, SLOTS, CW), F32),
            pltpu.VMEM((2, SLOTS, CW), F32),
            pltpu.VMEM((2, SLOTS, 2 * K), BF16),
            pltpu.VMEM((SLOTS, CW), F32),
            pltpu.VMEM((STEPS - 2, DS, K), F32),
            pltpu.VMEM((STEPS - 2, DS, K), F32),
            pltpu.VMEM((STEPS - 2, DS, K), F32),
            pltpu.VMEM((STEPS - 2, DS, K), F32),
            pltpu.VMEM((2, DS, K), F32),
            pltpu.VMEM((NZ, 4, 1, 128), F32),
            pltpu.VMEM((NZ, 4, 1, 128), F32),
            pltpu.VMEM((4, 1, 128), F32),
            pltpu.VMEM((NL, 1, 128), F32),
            pltpu.VMEM((NL, 8, 128), F32),
            pltpu.VMEM((NL, 8, 128), F32),
            pltpu.VMEM((NL, 8, 128), F32),
            pltpu.VMEM((NL, 8, 128), F32),
            pltpu.VMEM((8, 128), F32),
            pltpu.VMEM((NL, 1, 128), F32),
            pltpu.VMEM((NL, 1, 128), F32),
            dma((4,)),
            dma((2,)),
            dma((STEPS,)),
            dma((STEPS,)),
            dma((2,)),
            dma((STEPS - 2,)),
            dma((STEPS - 2,)),
            dma((2,)),
            dma((2,)),
            dma((2,)),
            dma((2,)),
            dma((2,)),
            dma((2,)),
        ],
        compiler_params=pltpu.CompilerParams(
            collective_id=0, has_side_effects=True, vmem_limit_bytes=56 * 2**20
        ),
    )(
        valid_rows,
        list_owner.T,
        list_slot.reshape(1, -1),
        pq_codes.T,
        memory_rows,
        centroids,
        codebook.transpose(0, 2, 1),
    )
    newcb, err = pl.pallas_call(
        hand_over,
        out_shape=(
            jax.ShapeDtypeStruct((2, DS, K), F32),
            jax.ShapeDtypeStruct((1, ROWS), F32),
        ),
        in_specs=[vmem, vmem],
        out_specs=(vmem, vmem),
    )(newcb, err)
    return newcb.transpose(0, 2, 1), err.reshape(-1)


def solution(mesh):
    in_specs = (
        P(("list", "rep"), None),
        P(("list", "rep"), None),
        P(("list", "rep")),
        P(("list", "rep"), None),
        P(("list", "rep")),
        P("list", None),
        P(),
    )
    out_specs = (P("rep", None, None), P(("list", "rep")))
    return jax.shard_map(body, mesh=mesh, in_specs=in_specs, out_specs=out_specs, check_vma=False)
```

```python
import functools

import jax
import jax.numpy as jnp
from jax import lax
from jax.experimental import pallas as pl
from jax.experimental.pallas import tpu as pltpu
from jax.sharding import PartitionSpec as P

prior_weight = 4.0

D = 1024
M = 16
K = 256
DS = 64
ROWS = 256
LISTS = 2048
CAP = 32
NL = 32
NZ = 8
SLOTS = NL * CAP
CW = 128
STEPS = D // CW

F32 = jnp.float32
BF16 = jnp.bfloat16
MESH = pl.DeviceIdType.MESH


def iota(shape, axis):
    return lax.broadcasted_iota(jnp.int32, shape, axis)


def dot(a, b, ca, cb):
    return lax.dot_general(a, b, (((ca,), (cb,)), ((), ())), preferred_element_type=F32)


def onehot(mask):
    return jnp.where(mask, 1.0, 0.0).astype(BF16)


def kernel(
    valid,
    owner,
    slot,
    codes,
    rows_hbm,
    cent_hbm,
    cb_hbm,
    newcb,
    err_out,
    rows,
    cents,
    cb,
    cbd,
    place,
    pos_ref,
    mt_send,
    mt_recv,
    meta,
    pick,
    send,
    recv,
    cent,
    recon,
    ohc,
    err,
    zin,
    zout,
    sib_send,
    sib_recv,
    held,
    cz_send,
    cz_recv,
    cx_send,
    cx_recv,
    hand_send,
    hand_recv,
    rs_send,
    rs_recv,
    ag_send,
    et_send,
    et_recv,
    local_sem,
    meta_sem,
    data_ss,
    data_rs,
    z_sem,
    sib_ss,
    sib_rs,
    cz_sem,
    cx_sem,
    hand_sem,
    rs_sem,
    ag_sem,
    et_sem,
):
    me = lax.axis_index("list")
    z = lax.axis_index("rep")

    load_rows = pltpu.make_async_copy(rows_hbm, rows, local_sem.at[0])
    load_cb = pltpu.make_async_copy(cb_hbm, cb, local_sem.at[1])
    load_cents = pltpu.make_async_copy(cent_hbm, cents, local_sem.at[2])
    load_rows.start()
    load_cb.start()
    load_cents.start()

    barrier = pltpu.get_barrier_semaphore()

    def greet(k, c):
        pl.semaphore_signal(
            barrier, inc=1, device_id=(lax.rem(me + k, NL), z), device_id_type=MESH
        )
        return c

    def greet_z(k, c):
        pl.semaphore_signal(
            barrier, inc=1, device_id=(me, lax.rem(z + k, NZ)), device_id_type=MESH
        )
        return c

    def greet_planes(k, c):
        for step in (1, NZ - 1):
            pl.semaphore_signal(
                barrier,
                inc=1,
                device_id=(lax.rem(me + k, NL), lax.rem(z + step, NZ)),
                device_id_type=MESH,
            )
        return c

    lax.fori_loop(1, NL, greet, 0)
    lax.fori_loop(1, NZ, greet_z, 0)
    lax.fori_loop(1, NL, greet_planes, 0)

    def peer(k):
        return lax.rem(me + k, NL)

    def ring(steps):
        return min(steps, 4 - steps)

    offsets = [(dx, dy, dc) for dx in range(4) for dy in range(4) for dc in range(2)]
    offsets.sort(key=lambda o: -(ring(o[0]) + ring(o[1])))

    def far_first():
        x, y, c = me // 8, lax.rem(me // 2, 4), lax.rem(me, 2)
        for dx, dy, dc in offsets[:-2]:
            yield (lax.rem(x + dx, 4) * 4 + lax.rem(y + dy, 4)) * 2 + lax.rem(c + dc, 2)
        yield me + 1 - 2 * c

    def copy_to(src, dst, ssem, rsem, who, plane):
        return pltpu.make_async_remote_copy(
            src_ref=src,
            dst_ref=dst,
            send_sem=ssem,
            recv_sem=rsem,
            device_id=(who, plane),
            device_id_type=MESH,
        )

    def pair_at(u, h):
        return lax.rem(z + (3 - u if h else 4 + u), NZ)

    def column(u, h):
        return pl.multiple_of(pair_at(u, h) * CW, CW)

    live = iota((1, ROWS), 1) < valid[0]
    own = jnp.where(live, owner[...], NL)
    named = iota((NL, ROWS), 0) == own
    named_f = jnp.where(named, 1.0, 0.0)
    earlier = onehot(iota((ROWS, ROWS), 0) < iota((ROWS, ROWS), 1))
    before = dot(named_f.astype(BF16), earlier, 1, 0)
    rank = jnp.sum(before * named_f, axis=0, keepdims=True)
    pos = jnp.where(live, own.astype(F32) * CAP + rank, -1.0)
    pos_ref[...] = pos

    def quarter(q):
        i = iota((ROWS, ROWS), 0)
        return ((i // 8) * CAP + q * 8 + i % 8).astype(F32)

    codes_f = jnp.where(live, (codes[...] + 1).astype(F32), 0.0)
    low = (slot[...] % 256).astype(F32)
    high = (slot[...] // 256 + 1).astype(F32)
    which = iota((16, ROWS), 0)
    tail = jnp.where(which == 0, low, jnp.where(which == 1, high, 0.0))
    tail = jnp.where(live, tail, 0.0)
    meta_t = jnp.concatenate([codes_f, tail], axis=0).astype(BF16)
    blank = jnp.zeros((32, ROWS), BF16)
    packed = jnp.zeros((ROWS, 128), F32)
    for q in range(4):
        shifted = jnp.concatenate([meta_t if i == q else blank for i in range(4)], axis=0)
        packed += dot(onehot(quarter(q) == pos), shifted, 1, 1)
    mt_send[...] = packed
    for b in range(4):
        place[pl.ds(b * 256, 256), :] = onehot((iota((256, ROWS), 0) + b * 256).astype(F32) == pos)

    err[...] = jnp.zeros((SLOTS, CW), F32)

    load_rows.wait()

    def bucket(v):
        first = 2 * v
        both = jnp.concatenate(
            [rows[:, pl.ds(column(v, 0), CW)], rows[:, pl.ds(column(v, 1), CW)]], axis=1
        )
        for b in range(4):
            part = dot(place[pl.ds(b * 256, 256), :], both, 1, 0).astype(BF16)
            send[first, pl.ds(b * 256, 256), :] = part[:, :CW]
            send[first + 1, pl.ds(b * 256, 256), :] = part[:, CW:]

    bucket(0)
    pl.semaphore_wait(barrier, 3 * (NL - 1) + NZ - 1)

    def tile8(j):
        return pl.ds(pl.multiple_of(j * 8, 8), 8)

    def tile32(j):
        return pl.ds(pl.multiple_of(j * CAP, CAP), CAP)

    def start(v, h):
        c = 2 * v + h
        for j in far_first():
            copy_to(
                send.at[c, tile32(j)], recv.at[c, tile32(me)], data_ss.at[c], data_rs.at[c], j, z
            ).start()
        recv[c, tile32(me), :] = send[c, tile32(me), :]

    def send_meta(k, c):
        j = peer(k)
        copy_to(mt_send.at[tile8(j)], mt_recv.at[tile8(me)], meta_sem.at[0], meta_sem.at[1], j, z).start()
        return c

    lax.fori_loop(1, NL, send_meta, 0)
    mt_recv[tile8(me), :] = mt_send[tile8(me), :]


    start(0, 0)
    start(0, 1)

    eye = onehot(iota((ROWS, ROWS), 0) == iota((ROWS, ROWS), 1))
    natural = dot(eye, meta_t, 1, 1)
    code_lane = (iota((ROWS, K), 1) + 1).astype(F32)
    code_lane2 = (iota((1024, K), 1) + 1).astype(F32)
    ones = jnp.ones((16, ROWS), BF16)
    for m in range(M):
        tally = dot(ones, onehot(natural[:, m : m + 1] == code_lane), 1, 0)
        for h in range(2):
            cz_send[m // 2, (m % 2) * 2 + h] = tally[0:1, h * 128 : (h + 1) * 128]

    def send_cz(k, c):
        other = lax.rem(z + k, NZ)
        copy_to(cz_send.at[other], cz_recv.at[z], cz_sem.at[0], cz_sem.at[1], me, other).start()
        return c

    lax.fori_loop(1, NZ, send_cz, 0)
    cz_recv[z] = cz_send[z]

    load_cb.wait()
    for p in range(STEPS):
        none = jnp.zeros((DS, K), F32)
        top = jnp.concatenate([cb[2 * p], none], axis=1)
        bottom = jnp.concatenate([none, cb[2 * p + 1]], axis=1)
        block = jnp.concatenate([top, bottom], axis=0)
        coarse = block.astype(BF16)
        cbd[p, 0:CW, :] = coarse
        cbd[p, CW : 2 * CW, :] = (block - coarse.astype(F32)).astype(BF16)

    copy_to(
        mt_send.at[pl.ds(0, 248)], mt_recv.at[pl.ds(0, 248)], meta_sem.at[0], meta_sem.at[1], me, z
    ).wait_recv()
    got = mt_recv[...]
    for q in range(4):
        turned = got if q == 0 else pltpu.roll(got, 128 - 32 * q, 1)
        meta[:, q] = turned.reshape(NL, 8, 128)

    def meta_rows(b):
        return meta[pl.ds(b * 32, 32)].reshape(1024, 128)

    def build_pick(b, c):
        m = meta_rows(b)
        wanted = m[:, 17:18] * 256.0 + m[:, 16:17] - 256.0
        for t in range(4):
            lanes = (iota((1024, 512), 1) + t * 512).astype(F32)
            pick[pl.ds(b * 1024, 1024), t * 512 : (t + 1) * 512] = onehot(wanted == lanes)
        return c

    lax.fori_loop(0, 1, build_pick, 0)
    load_cents.wait()

    core = lax.rem(me, 2)
    sibling = me + 1 - 2 * core

    def share(s, mine, theirs):
        zout[s] = mine
        sib_send[s] = theirs
        copy_to(sib_send.at[s], sib_recv.at[s], sib_ss.at[s], sib_rs.at[s], sibling, z).start()

    def forward(u, h):
        s = 2 * u + h
        copy_to(sib_send.at[s], sib_recv.at[s], sib_ss.at[s], sib_rs.at[s], sibling, z).wait_recv()
        zout[s] = zout[s] + sib_recv[s]
        copy_to(zout.at[s], zin.at[s], z_sem.at[0], z_sem.at[1], me, pair_at(u, h)).start()

    def pass_counts():
        copy_to(
            cz_send.at[pl.ds(0, NZ - 1)], cz_recv.at[pl.ds(0, NZ - 1)], cz_sem.at[0], cz_sem.at[1], me, z
        ).wait_recv()
        cx_send[...] = jnp.sum(cz_recv[...], axis=0)

        def send_cx(k, c):
            j = peer(k)
            piece = (j // 16) * 2 + lax.rem(j, 2)
            copy_to(cx_send.at[piece], cx_recv.at[me], cx_sem.at[0], cx_sem.at[1], j, z).start()
            return c

        lax.fori_loop(1, NL, send_cx, 0)
        cx_recv[me] = cx_send[(me // 16) * 2 + lax.rem(me, 2)]

    def piece_of(sums, i):
        a, d, h = i // 16, (i // 2) % 8, i % 2
        return sums[a][d * 8 : (d + 1) * 8, h * 128 : (h + 1) * 128]

    def send_hand(k, c):
        j = peer(k)
        copy_to(
            hand_send.at[j], hand_recv.at[me], hand_sem.at[0], hand_sem.at[1], j, pair_at(3, 0)
        ).start()
        return c

    def two_steps(u, carry):
        @pl.when(u < 3)
        def _():
            bucket(u + 1)
            start(u + 1, 0)

        table = jnp.concatenate(
            [cents[:, pl.ds(column(u, 0), CW)], cents[:, pl.ds(column(u, 1), CW)]], axis=1
        )

        def ahead(b, c):
            r = pl.ds(b * 1024, 1024)
            centre = dot(pick[r, :], table, 1, 0)
            m = meta_rows(b)
            for h in range(2):
                p = pair_at(u, h)
                cent[h, r, :] = centre[:, h * CW : (h + 1) * CW]
                turned = pltpu.roll(m, lax.rem(128 - 2 * p, 128), 1)
                hot = jnp.concatenate(
                    [onehot(turned[:, 0:1] == code_lane2), onehot(turned[:, 1:2] == code_lane2)], axis=1
                )
                ohc[h, r, :] = hot
                value = dot(hot, cbd[p], 1, 1)
                recon[h, r, :] = value[:, :CW] + value[:, CW:]
            return c

        lax.fori_loop(0, 1, ahead, 0)

        @pl.when(u > 0)
        def _():
            forward(u - 1, 0)
            forward(u - 1, 1)

        pl.when(u == 1)(pass_counts)

        for h in range(2):
            s = 2 * u + h
            copy_to(
                send.at[s, pl.ds(0, SLOTS - CAP)],
                recv.at[s, pl.ds(0, SLOTS - CAP)],
                data_ss.at[s],
                data_rs.at[s],
                me,
                z,
            ).wait_recv()

            total = jnp.zeros((CW, 2 * K), F32)
            for b in range(4):
                r = pl.ds(b * 256, 256)
                residual = recv[s, r, :].astype(F32) - cent[h, r, :]
                gap = residual - recon[h, r, :]
                err[r, :] += gap * gap
                total += dot(residual.astype(BF16), ohc[h, r, :], 0, 0)
            first, second = total[:DS, :K], total[DS:, K:]
            mine = jnp.where(core == 0, first, second)
            theirs = jnp.where(core == 0, second, first)

            @pl.when(u < 3)
            def _():
                share(s, mine, theirs)
                if h == 0:
                    start(u + 1, 1)

            @pl.when(u == 3)
            def _():
                if h == 1:
                    held[0] = first
                    held[1] = second
                else:
                    for i in range(NL):
                        hand_send[i] = piece_of((first, second), i)
                    lax.fori_loop(0, NL, send_hand, 0)

        return carry

    lax.fori_loop(0, STEPS // 2, two_steps, 0)

    z_all = copy_to(
        zout, zin, z_sem.at[0], z_sem.at[1], me, z
    )
    z_all.wait_recv()
    others = jnp.sum(zin[...], axis=0)
    plane_sum = [held[a] + jnp.where(core == a, others, 0.0) for a in range(2)]

    for i in range(NL):
        rs_send[i] = piece_of(plane_sum, i)

    for j in far_first():
        copy_to(rs_send.at[j], rs_recv.at[me], rs_sem.at[0], rs_sem.at[1], j, z).start()
    rs_recv[me] = rs_send[me]

    summed = (jnp.sum(err[...], axis=1, keepdims=True) * (1.0 / D)).reshape(NL, 4, 8, 1)
    lane = iota((NL, 8, 128), 2)
    tiles = jnp.zeros((NL, 8, 128), F32)
    for q in range(4):
        tiles = jnp.where(lane // 32 == q, summed[:, q], tiles)
    tiles = jnp.where((lane % 32) // 4 == iota((NL, 8, 128), 1), tiles, 0.0)
    et_send[...] = jnp.sum(tiles, axis=1, keepdims=True)

    def send_et(k, c):
        j = peer(k)
        copy_to(et_send.at[j], et_recv.at[me], et_sem.at[0], et_sem.at[1], j, z).start()
        return c

    lax.fori_loop(1, NL, send_et, 0)
    et_recv[me] = et_send[me]

    def wait_all(src, dst, sem):
        whole = copy_to(src, dst, sem.at[0], sem.at[1], me, z)
        return whole

    first31 = pl.ds(0, NL - 1)
    cx_all = wait_all(cx_recv.at[first31], cx_recv.at[first31], cx_sem)
    rs_all = wait_all(rs_send.at[first31], rs_recv.at[first31], rs_sem)
    hand_all = wait_all(hand_send, hand_recv, hand_sem)
    ag_all = wait_all(rs_send.at[first31], rs_recv.at[first31], ag_sem)
    et_all = wait_all(et_send.at[first31], et_recv.at[first31], et_sem)

    cx_all.wait_recv()
    count = jnp.sum(cx_recv[...], axis=0)
    rs_all.wait_recv()
    hand_all.wait_recv()
    total = jnp.sum(rs_recv[...] + hand_recv[...], axis=0)

    def place_of(ref, i):
        rows_at = pl.ds(pl.multiple_of(lax.rem(i // 2, 8) * 8, 8), 8)
        return ref.at[i // 16, rows_at, pl.ds(pl.multiple_of(lax.rem(i, 2) * 128, 128), 128)]

    old = cb[
        2 * z + me // 16,
        pl.ds(pl.multiple_of(lax.rem(me // 2, 8) * 8, 8), 8),
        pl.ds(pl.multiple_of(lax.rem(me, 2) * 128, 128), 128),
    ]
    ag_send[...] = (total + prior_weight * old) / (count + prior_weight)

    for j in far_first():
        copy_to(ag_send, place_of(newcb, me), ag_sem.at[0], ag_sem.at[1], j, z).start()
    own_piece = pltpu.make_async_copy(ag_send, place_of(newcb, me), local_sem.at[3])
    own_piece.start()

    et_all.wait_recv()
    rest = et_recv[...].reshape(NL, 128)
    holder = pos_ref[...]
    owner_of = jnp.floor(holder * (1.0 / CAP))
    at = onehot(iota((128, ROWS), 0).astype(F32) == (holder - owner_of * CAP) * 4.0)
    picked = jnp.zeros((NL, ROWS), F32)
    for _ in range(3):
        part = rest.astype(BF16)
        rest = rest - part.astype(F32)
        picked += dot(part, at, 1, 0)
    belongs = iota((NL, ROWS), 0).astype(F32) == owner_of
    err_out[...] = jnp.sum(jnp.where(belongs, picked, 0.0), axis=0, keepdims=True)

    ag_all.wait_recv()
    own_piece.wait()

    copy_to(
        mt_send.at[pl.ds(0, 248)], mt_recv.at[pl.ds(0, 248)], meta_sem.at[0], meta_sem.at[1], me, z
    ).wait_send()
    copy_to(
        cz_send.at[pl.ds(0, NZ - 1)], cz_recv.at[pl.ds(0, NZ - 1)], cz_sem.at[0], cz_sem.at[1], me, z
    ).wait_send()

    def drain(s, c):
        copy_to(
            send.at[s, pl.ds(0, SLOTS - CAP)],
            recv.at[s, pl.ds(0, SLOTS - CAP)],
            data_ss.at[s],
            data_rs.at[s],
            me,
            z,
        ).wait_send()
        return c

    lax.fori_loop(0, STEPS, drain, 0)

    z_all.wait_send()

    def drain_share(i, c):
        copy_to(sib_send.at[i], sib_recv.at[i], sib_ss.at[i], sib_rs.at[i], sibling, z).wait_send()
        return c

    lax.fori_loop(0, STEPS - 2, drain_share, 0)
    cx_all.wait_send()
    hand_all.wait_send()
    rs_all.wait_send()
    et_all.wait_send()
    ag_all.wait_send()


def hand_over(newcb_in, err_in, newcb_out, err_out):
    newcb_out[...] = newcb_in[...]
    err_out[...] = err_in[...]


def body(memory_rows, list_owner, list_slot, pq_codes, valid_rows, centroids, codebook):
    vmem = pl.BlockSpec(memory_space=pltpu.VMEM)
    anywhere = pl.BlockSpec(memory_space=pl.ANY)
    dma = pltpu.SemaphoreType.DMA
    newcb, err = pl.pallas_call(
        kernel,
        out_shape=(
            jax.ShapeDtypeStruct((2, DS, K), F32),
            jax.ShapeDtypeStruct((1, ROWS), F32),
        ),
        in_specs=[pl.BlockSpec(memory_space=pltpu.SMEM), vmem, vmem, vmem, anywhere, anywhere, anywhere],
        out_specs=(anywhere, vmem),
        scratch_shapes=[
            pltpu.VMEM((ROWS, D), BF16),
            pltpu.VMEM((LISTS, D), BF16),
            pltpu.VMEM((M, DS, K), F32),
            pltpu.VMEM((STEPS, 2 * CW, 2 * K), BF16),
            pltpu.VMEM((SLOTS, ROWS), BF16),
            pltpu.VMEM((1, ROWS), F32),
            pltpu.VMEM((NL * 8, 128), F32),
            pltpu.VMEM((NL * 8, 128), F32),
            pltpu.VMEM((NL, 4, 8, 128), F32),
            pltpu.VMEM((SLOTS, LISTS), BF16),
            pltpu.VMEM((STEPS, SLOTS, CW), BF16),
            pltpu.VMEM((STEPS, SLOTS, CW), BF16),
            pltpu.VMEM((2, SLOTS, CW), F32),
            pltpu.VMEM((2, SLOTS, CW), F32),
            pltpu.VMEM((2, SLOTS, 2 * K), BF16),
            pltpu.VMEM((SLOTS, CW), F32),
            pltpu.VMEM((STEPS - 2, DS, K), F32),
            pltpu.VMEM((STEPS - 2, DS, K), F32),
            pltpu.VMEM((STEPS - 2, DS, K), F32),
            pltpu.VMEM((STEPS - 2, DS, K), F32),
            pltpu.VMEM((2, DS, K), F32),
            pltpu.VMEM((NZ, 4, 1, 128), F32),
            pltpu.VMEM((NZ, 4, 1, 128), F32),
            pltpu.VMEM((4, 1, 128), F32),
            pltpu.VMEM((NL, 1, 128), F32),
            pltpu.VMEM((NL, 8, 128), F32),
            pltpu.VMEM((NL, 8, 128), F32),
            pltpu.VMEM((NL, 8, 128), F32),
            pltpu.VMEM((NL, 8, 128), F32),
            pltpu.VMEM((8, 128), F32),
            pltpu.VMEM((NL, 1, 128), F32),
            pltpu.VMEM((NL, 1, 128), F32),
            dma((4,)),
            dma((2,)),
            dma((STEPS,)),
            dma((STEPS,)),
            dma((2,)),
            dma((STEPS - 2,)),
            dma((STEPS - 2,)),
            dma((2,)),
            dma((2,)),
            dma((2,)),
            dma((2,)),
            dma((2,)),
            dma((2,)),
        ],
        compiler_params=pltpu.CompilerParams(
            collective_id=0, has_side_effects=True, vmem_limit_bytes=56 * 2**20
        ),
    )(
        valid_rows,
        list_owner.T,
        list_slot.reshape(1, -1),
        pq_codes.T,
        memory_rows,
        centroids,
        codebook.transpose(0, 2, 1),
    )
    newcb, err = pl.pallas_call(
        hand_over,
        out_shape=(
            jax.ShapeDtypeStruct((2, DS, K), F32),
            jax.ShapeDtypeStruct((1, ROWS), F32),
        ),
        in_specs=[vmem, vmem],
        out_specs=(vmem, vmem),
    )(newcb, err)
    return newcb.transpose(0, 2, 1), err.reshape(-1)


def solution(mesh):
    in_specs = (
        P(("list", "rep"), None),
        P(("list", "rep"), None),
        P(("list", "rep")),
        P(("list", "rep"), None),
        P(("list", "rep")),
        P("list", None),
        P(),
    )
    out_specs = (P("rep", None, None), P(("list", "rep")))
    return jax.shard_map(body, mesh=mesh, in_specs=in_specs, out_specs=out_specs, check_vma=False)
```

```python
import functools

import jax
import jax.numpy as jnp
from jax import lax
from jax.experimental import pallas as pl
from jax.experimental.pallas import tpu as pltpu
from jax.sharding import PartitionSpec as P

prior_weight = 4.0

D = 1024
M = 16
K = 256
DS = 64
ROWS = 256
LISTS = 2048
CAP = 32
NL = 32
NZ = 8
SLOTS = NL * CAP
CW = 128
STEPS = D // CW

F32 = jnp.float32
BF16 = jnp.bfloat16
MESH = pl.DeviceIdType.MESH


def iota(shape, axis):
    return lax.broadcasted_iota(jnp.int32, shape, axis)


def dot(a, b, ca, cb):
    return lax.dot_general(a, b, (((ca,), (cb,)), ((), ())), preferred_element_type=F32)


def onehot(mask):
    return jnp.where(mask, 1.0, 0.0).astype(BF16)


def kernel(
    valid,
    owner,
    slot,
    codes,
    rows_hbm,
    cent_hbm,
    cb_hbm,
    newcb,
    err_out,
    rows,
    cents,
    cb,
    cbd,
    place,
    pos_ref,
    mt_send,
    mt_recv,
    meta,
    pick,
    send,
    recv,
    cent,
    recon,
    ohc,
    err,
    zin,
    zout,
    sib_send,
    sib_recv,
    held,
    cz_send,
    cz_recv,
    cx_send,
    cx_recv,
    hand_send,
    hand_recv,
    rs_send,
    rs_recv,
    ag_send,
    et_send,
    et_recv,
    local_sem,
    meta_sem,
    data_ss,
    data_rs,
    z_sem,
    sib_ss,
    sib_rs,
    cz_sem,
    cx_sem,
    hand_sem,
    rs_sem,
    ag_sem,
    et_sem,
):
    me = lax.axis_index("list")
    z = lax.axis_index("rep")

    load_rows = pltpu.make_async_copy(rows_hbm, rows, local_sem.at[0])
    load_cb = pltpu.make_async_copy(cb_hbm, cb, local_sem.at[1])
    load_cents = pltpu.make_async_copy(cent_hbm, cents, local_sem.at[2])
    load_rows.start()
    load_cb.start()
    load_cents.start()

    barrier = pltpu.get_barrier_semaphore()

    def greet(k, c):
        pl.semaphore_signal(
            barrier, inc=1, device_id=(lax.rem(me + k, NL), z), device_id_type=MESH
        )
        return c

    def greet_z(k, c):
        pl.semaphore_signal(
            barrier, inc=1, device_id=(me, lax.rem(z + k, NZ)), device_id_type=MESH
        )
        return c

    def greet_planes(k, c):
        for step in (1, NZ - 1):
            pl.semaphore_signal(
                barrier,
                inc=1,
                device_id=(lax.rem(me + k, NL), lax.rem(z + step, NZ)),
                device_id_type=MESH,
            )
        return c

    lax.fori_loop(1, NL, greet, 0)
    lax.fori_loop(1, NZ, greet_z, 0)
    lax.fori_loop(1, NL, greet_planes, 0)

    def peer(k):
        return lax.rem(me + k, NL)

    def ring(steps):
        return min(steps, 4 - steps)

    offsets = [(dx, dy, dc) for dx in range(4) for dy in range(4) for dc in range(2)]
    offsets.sort(key=lambda o: -(ring(o[0]) + ring(o[1])))

    def far_first():
        x, y, c = me // 8, lax.rem(me // 2, 4), lax.rem(me, 2)
        for dx, dy, dc in offsets[:-2]:
            yield (lax.rem(x + dx, 4) * 4 + lax.rem(y + dy, 4)) * 2 + lax.rem(c + dc, 2)
        yield me + 1 - 2 * c

    def copy_to(src, dst, ssem, rsem, who, plane):
        return pltpu.make_async_remote_copy(
            src_ref=src,
            dst_ref=dst,
            send_sem=ssem,
            recv_sem=rsem,
            device_id=(who, plane),
            device_id_type=MESH,
        )

    def pair_at(u, h):
        return lax.rem(z + (3 - u if h else 4 + u), NZ)

    def column(u, h):
        return pl.multiple_of(pair_at(u, h) * CW, CW)

    live = iota((1, ROWS), 1) < valid[0]
    own = jnp.where(live, owner[...], NL)
    named = iota((NL, ROWS), 0) == own
    named_f = jnp.where(named, 1.0, 0.0)
    earlier = onehot(iota((ROWS, ROWS), 0) < iota((ROWS, ROWS), 1))
    before = dot(named_f.astype(BF16), earlier, 1, 0)
    rank = jnp.sum(before * named_f, axis=0, keepdims=True)
    pos = jnp.where(live, own.astype(F32) * CAP + rank, -1.0)
    pos_ref[...] = pos

    def quarter(q):
        i = iota((ROWS, ROWS), 0)
        return ((i // 8) * CAP + q * 8 + i % 8).astype(F32)

    codes_f = jnp.where(live, (codes[...] + 1).astype(F32), 0.0)
    low = (slot[...] % 256).astype(F32)
    high = (slot[...] // 256 + 1).astype(F32)
    which = iota((16, ROWS), 0)
    tail = jnp.where(which == 0, low, jnp.where(which == 1, high, 0.0))
    tail = jnp.where(live, tail, 0.0)
    meta_t = jnp.concatenate([codes_f, tail], axis=0).astype(BF16)
    blank = jnp.zeros((32, ROWS), BF16)
    packed = jnp.zeros((ROWS, 128), F32)
    for q in range(4):
        shifted = jnp.concatenate([meta_t if i == q else blank for i in range(4)], axis=0)
        packed += dot(onehot(quarter(q) == pos), shifted, 1, 1)
    mt_send[...] = packed
    for b in range(4):
        place[pl.ds(b * 256, 256), :] = onehot((iota((256, ROWS), 0) + b * 256).astype(F32) == pos)

    err[...] = jnp.zeros((SLOTS, CW), F32)

    load_rows.wait()

    def bucket(v):
        first = 2 * v
        both = jnp.concatenate(
            [rows[:, pl.ds(column(v, 0), CW)], rows[:, pl.ds(column(v, 1), CW)]], axis=1
        )
        for b in range(4):
            part = dot(place[pl.ds(b * 256, 256), :], both, 1, 0).astype(BF16)
            send[first, pl.ds(b * 256, 256), :] = part[:, :CW]
            send[first + 1, pl.ds(b * 256, 256), :] = part[:, CW:]

    bucket(0)
    pl.semaphore_wait(barrier, 3 * (NL - 1) + NZ - 1)

    def tile8(j):
        return pl.ds(pl.multiple_of(j * 8, 8), 8)

    def tile32(j):
        return pl.ds(pl.multiple_of(j * CAP, CAP), CAP)

    def start(v, h):
        c = 2 * v + h
        for j in far_first():
            copy_to(
                send.at[c, tile32(j)], recv.at[c, tile32(me)], data_ss.at[c], data_rs.at[c], j, z
            ).start()
        recv[c, tile32(me), :] = send[c, tile32(me), :]

    for j in far_first():
        copy_to(
            mt_send.at[tile8(j)], mt_recv.at[tile8(me)], meta_sem.at[0], meta_sem.at[1], j, z
        ).start()
    mt_recv[tile8(me), :] = mt_send[tile8(me), :]


    start(0, 0)
    start(0, 1)

    eye = onehot(iota((ROWS, ROWS), 0) == iota((ROWS, ROWS), 1))
    natural = dot(eye, meta_t, 1, 1)
    code_lane = (iota((ROWS, K), 1) + 1).astype(F32)
    code_lane2 = (iota((1024, K), 1) + 1).astype(F32)
    ones = jnp.ones((16, ROWS), BF16)
    for m in range(M):
        tally = dot(ones, onehot(natural[:, m : m + 1] == code_lane), 1, 0)
        for h in range(2):
            cz_send[m // 2, (m % 2) * 2 + h] = tally[0:1, h * 128 : (h + 1) * 128]

    def send_cz(k, c):
        other = lax.rem(z + k, NZ)
        copy_to(cz_send.at[other], cz_recv.at[z], cz_sem.at[0], cz_sem.at[1], me, other).start()
        return c

    lax.fori_loop(1, NZ, send_cz, 0)
    cz_recv[z] = cz_send[z]

    load_cb.wait()
    for p in range(STEPS):
        none = jnp.zeros((DS, K), F32)
        top = jnp.concatenate([cb[2 * p], none], axis=1)
        bottom = jnp.concatenate([none, cb[2 * p + 1]], axis=1)
        block = jnp.concatenate([top, bottom], axis=0)
        coarse = block.astype(BF16)
        cbd[p, 0:CW, :] = coarse
        cbd[p, CW : 2 * CW, :] = (block - coarse.astype(F32)).astype(BF16)

    copy_to(
        mt_send.at[pl.ds(0, 248)], mt_recv.at[pl.ds(0, 248)], meta_sem.at[0], meta_sem.at[1], me, z
    ).wait_recv()
    got = mt_recv[...]
    for q in range(4):
        turned = got if q == 0 else pltpu.roll(got, 128 - 32 * q, 1)
        meta[:, q] = turned.reshape(NL, 8, 128)

    def meta_rows(b):
        return meta[pl.ds(b * 32, 32)].reshape(1024, 128)

    def build_pick(b, c):
        m = meta_rows(b)
        wanted = m[:, 17:18] * 256.0 + m[:, 16:17] - 256.0
        for t in range(4):
            lanes = (iota((1024, 512), 1) + t * 512).astype(F32)
            pick[pl.ds(b * 1024, 1024), t * 512 : (t + 1) * 512] = onehot(wanted == lanes)
        return c

    lax.fori_loop(0, 1, build_pick, 0)
    load_cents.wait()

    core = lax.rem(me, 2)
    sibling = me + 1 - 2 * core

    def share(s, mine, theirs):
        zout[s] = mine
        sib_send[s] = theirs
        copy_to(sib_send.at[s], sib_recv.at[s], sib_ss.at[s], sib_rs.at[s], sibling, z).start()

    def forward(u, h):
        s = 2 * u + h
        copy_to(sib_send.at[s], sib_recv.at[s], sib_ss.at[s], sib_rs.at[s], sibling, z).wait_recv()
        zout[s] = zout[s] + sib_recv[s]
        copy_to(zout.at[s], zin.at[s], z_sem.at[0], z_sem.at[1], me, pair_at(u, h)).start()

    def pass_counts():
        copy_to(
            cz_send.at[pl.ds(0, NZ - 1)], cz_recv.at[pl.ds(0, NZ - 1)], cz_sem.at[0], cz_sem.at[1], me, z
        ).wait_recv()
        cx_send[...] = jnp.sum(cz_recv[...], axis=0)

        def send_cx(k, c):
            j = peer(k)
            piece = (j // 16) * 2 + lax.rem(j, 2)
            copy_to(cx_send.at[piece], cx_recv.at[me], cx_sem.at[0], cx_sem.at[1], j, z).start()
            return c

        lax.fori_loop(1, NL, send_cx, 0)
        cx_recv[me] = cx_send[(me // 16) * 2 + lax.rem(me, 2)]

    def piece_of(sums, i):
        a, d, h = i // 16, (i // 2) % 8, i % 2
        return sums[a][d * 8 : (d + 1) * 8, h * 128 : (h + 1) * 128]

    def send_hand(k, c):
        j = peer(k)
        copy_to(
            hand_send.at[j], hand_recv.at[me], hand_sem.at[0], hand_sem.at[1], j, pair_at(3, 0)
        ).start()
        return c

    def two_steps(u, carry):
        @pl.when(u < 3)
        def _():
            bucket(u + 1)
            start(u + 1, 0)

        table = jnp.concatenate(
            [cents[:, pl.ds(column(u, 0), CW)], cents[:, pl.ds(column(u, 1), CW)]], axis=1
        )

        def ahead(b, c):
            r = pl.ds(b * 1024, 1024)
            centre = dot(pick[r, :], table, 1, 0)
            m = meta_rows(b)
            for h in range(2):
                p = pair_at(u, h)
                cent[h, r, :] = centre[:, h * CW : (h + 1) * CW]
                turned = pltpu.roll(m, lax.rem(128 - 2 * p, 128), 1)
                hot = jnp.concatenate(
                    [onehot(turned[:, 0:1] == code_lane2), onehot(turned[:, 1:2] == code_lane2)], axis=1
                )
                ohc[h, r, :] = hot
                value = dot(hot, cbd[p], 1, 1)
                recon[h, r, :] = value[:, :CW] + value[:, CW:]
            return c

        lax.fori_loop(0, 1, ahead, 0)

        @pl.when(u > 0)
        def _():
            forward(u - 1, 0)
            forward(u - 1, 1)

        pl.when(u == 1)(pass_counts)

        for h in range(2):
            s = 2 * u + h
            copy_to(
                send.at[s, pl.ds(0, SLOTS - CAP)],
                recv.at[s, pl.ds(0, SLOTS - CAP)],
                data_ss.at[s],
                data_rs.at[s],
                me,
                z,
            ).wait_recv()

            total = jnp.zeros((CW, 2 * K), F32)
            for b in range(4):
                r = pl.ds(b * 256, 256)
                residual = recv[s, r, :].astype(F32) - cent[h, r, :]
                gap = residual - recon[h, r, :]
                err[r, :] += gap * gap
                total += dot(residual.astype(BF16), ohc[h, r, :], 0, 0)
            first, second = total[:DS, :K], total[DS:, K:]
            mine = jnp.where(core == 0, first, second)
            theirs = jnp.where(core == 0, second, first)

            @pl.when(u < 3)
            def _():
                share(s, mine, theirs)
                if h == 0:
                    start(u + 1, 1)

            @pl.when(u == 3)
            def _():
                if h == 1:
                    held[0] = first
                    held[1] = second
                else:
                    for i in range(NL):
                        hand_send[i] = piece_of((first, second), i)
                    lax.fori_loop(0, NL, send_hand, 0)

        return carry

    lax.fori_loop(0, STEPS // 2, two_steps, 0)

    z_all = copy_to(
        zout, zin, z_sem.at[0], z_sem.at[1], me, z
    )
    z_all.wait_recv()
    others = jnp.sum(zin[...], axis=0)
    plane_sum = [held[a] + jnp.where(core == a, others, 0.0) for a in range(2)]

    for i in range(NL):
        rs_send[i] = piece_of(plane_sum, i)

    for j in far_first():
        copy_to(rs_send.at[j], rs_recv.at[me], rs_sem.at[0], rs_sem.at[1], j, z).start()
    rs_recv[me] = rs_send[me]

    summed = (jnp.sum(err[...], axis=1, keepdims=True) * (1.0 / D)).reshape(NL, 4, 8, 1)
    lane = iota((NL, 8, 128), 2)
    tiles = jnp.zeros((NL, 8, 128), F32)
    for q in range(4):
        tiles = jnp.where(lane // 32 == q, summed[:, q], tiles)
    tiles = jnp.where((lane % 32) // 4 == iota((NL, 8, 128), 1), tiles, 0.0)
    et_send[...] = jnp.sum(tiles, axis=1, keepdims=True)

    def send_et(k, c):
        j = peer(k)
        copy_to(et_send.at[j], et_recv.at[me], et_sem.at[0], et_sem.at[1], j, z).start()
        return c

    lax.fori_loop(1, NL, send_et, 0)
    et_recv[me] = et_send[me]

    def wait_all(src, dst, sem):
        whole = copy_to(src, dst, sem.at[0], sem.at[1], me, z)
        return whole

    first31 = pl.ds(0, NL - 1)
    cx_all = wait_all(cx_recv.at[first31], cx_recv.at[first31], cx_sem)
    rs_all = wait_all(rs_send.at[first31], rs_recv.at[first31], rs_sem)
    hand_all = wait_all(hand_send, hand_recv, hand_sem)
    ag_all = wait_all(rs_send.at[first31], rs_recv.at[first31], ag_sem)
    et_all = wait_all(et_send.at[first31], et_recv.at[first31], et_sem)

    cx_all.wait_recv()
    count = jnp.sum(cx_recv[...], axis=0)
    rs_all.wait_recv()
    hand_all.wait_recv()
    total = jnp.sum(rs_recv[...] + hand_recv[...], axis=0)

    def place_of(ref, i):
        rows_at = pl.ds(pl.multiple_of(lax.rem(i // 2, 8) * 8, 8), 8)
        return ref.at[i // 16, rows_at, pl.ds(pl.multiple_of(lax.rem(i, 2) * 128, 128), 128)]

    old = cb[
        2 * z + me // 16,
        pl.ds(pl.multiple_of(lax.rem(me // 2, 8) * 8, 8), 8),
        pl.ds(pl.multiple_of(lax.rem(me, 2) * 128, 128), 128),
    ]
    ag_send[...] = (total + prior_weight * old) / (count + prior_weight)

    for j in far_first():
        copy_to(ag_send, place_of(newcb, me), ag_sem.at[0], ag_sem.at[1], j, z).start()
    own_piece = pltpu.make_async_copy(ag_send, place_of(newcb, me), local_sem.at[3])
    own_piece.start()

    et_all.wait_recv()
    rest = et_recv[...].reshape(NL, 128)
    holder = pos_ref[...]
    owner_of = jnp.floor(holder * (1.0 / CAP))
    at = onehot(iota((128, ROWS), 0).astype(F32) == (holder - owner_of * CAP) * 4.0)
    picked = jnp.zeros((NL, ROWS), F32)
    for _ in range(3):
        part = rest.astype(BF16)
        rest = rest - part.astype(F32)
        picked += dot(part, at, 1, 0)
    belongs = iota((NL, ROWS), 0).astype(F32) == owner_of
    err_out[...] = jnp.sum(jnp.where(belongs, picked, 0.0), axis=0, keepdims=True)

    ag_all.wait_recv()
    own_piece.wait()

    copy_to(
        mt_send.at[pl.ds(0, 248)], mt_recv.at[pl.ds(0, 248)], meta_sem.at[0], meta_sem.at[1], me, z
    ).wait_send()
    copy_to(
        cz_send.at[pl.ds(0, NZ - 1)], cz_recv.at[pl.ds(0, NZ - 1)], cz_sem.at[0], cz_sem.at[1], me, z
    ).wait_send()

    def drain(s, c):
        copy_to(
            send.at[s, pl.ds(0, SLOTS - CAP)],
            recv.at[s, pl.ds(0, SLOTS - CAP)],
            data_ss.at[s],
            data_rs.at[s],
            me,
            z,
        ).wait_send()
        return c

    lax.fori_loop(0, STEPS, drain, 0)

    z_all.wait_send()

    def drain_share(i, c):
        copy_to(sib_send.at[i], sib_recv.at[i], sib_ss.at[i], sib_rs.at[i], sibling, z).wait_send()
        return c

    lax.fori_loop(0, STEPS - 2, drain_share, 0)
    cx_all.wait_send()
    hand_all.wait_send()
    rs_all.wait_send()
    et_all.wait_send()
    ag_all.wait_send()


def hand_over(newcb_in, err_in, newcb_out, err_out):
    newcb_out[...] = newcb_in[...]
    err_out[...] = err_in[...]


def body(memory_rows, list_owner, list_slot, pq_codes, valid_rows, centroids, codebook):
    vmem = pl.BlockSpec(memory_space=pltpu.VMEM)
    anywhere = pl.BlockSpec(memory_space=pl.ANY)
    dma = pltpu.SemaphoreType.DMA
    newcb, err = pl.pallas_call(
        kernel,
        out_shape=(
            jax.ShapeDtypeStruct((2, DS, K), F32),
            jax.ShapeDtypeStruct((1, ROWS), F32),
        ),
        in_specs=[pl.BlockSpec(memory_space=pltpu.SMEM), vmem, vmem, vmem, anywhere, anywhere, anywhere],
        out_specs=(anywhere, vmem),
        scratch_shapes=[
            pltpu.VMEM((ROWS, D), BF16),
            pltpu.VMEM((LISTS, D), BF16),
            pltpu.VMEM((M, DS, K), F32),
            pltpu.VMEM((STEPS, 2 * CW, 2 * K), BF16),
            pltpu.VMEM((SLOTS, ROWS), BF16),
            pltpu.VMEM((1, ROWS), F32),
            pltpu.VMEM((NL * 8, 128), F32),
            pltpu.VMEM((NL * 8, 128), F32),
            pltpu.VMEM((NL, 4, 8, 128), F32),
            pltpu.VMEM((SLOTS, LISTS), BF16),
            pltpu.VMEM((STEPS, SLOTS, CW), BF16),
            pltpu.VMEM((STEPS, SLOTS, CW), BF16),
            pltpu.VMEM((2, SLOTS, CW), F32),
            pltpu.VMEM((2, SLOTS, CW), F32),
            pltpu.VMEM((2, SLOTS, 2 * K), BF16),
            pltpu.VMEM((SLOTS, CW), F32),
            pltpu.VMEM((STEPS - 2, DS, K), F32),
            pltpu.VMEM((STEPS - 2, DS, K), F32),
            pltpu.VMEM((STEPS - 2, DS, K), F32),
            pltpu.VMEM((STEPS - 2, DS, K), F32),
            pltpu.VMEM((2, DS, K), F32),
            pltpu.VMEM((NZ, 4, 1, 128), F32),
            pltpu.VMEM((NZ, 4, 1, 128), F32),
            pltpu.VMEM((4, 1, 128), F32),
            pltpu.VMEM((NL, 1, 128), F32),
            pltpu.VMEM((NL, 8, 128), F32),
            pltpu.VMEM((NL, 8, 128), F32),
            pltpu.VMEM((NL, 8, 128), F32),
            pltpu.VMEM((NL, 8, 128), F32),
            pltpu.VMEM((8, 128), F32),
            pltpu.VMEM((NL, 1, 128), F32),
            pltpu.VMEM((NL, 1, 128), F32),
            dma((4,)),
            dma((2,)),
            dma((STEPS,)),
            dma((STEPS,)),
            dma((2,)),
            dma((STEPS - 2,)),
            dma((STEPS - 2,)),
            dma((2,)),
            dma((2,)),
            dma((2,)),
            dma((2,)),
            dma((2,)),
            dma((2,)),
        ],
        compiler_params=pltpu.CompilerParams(
            collective_id=0, has_side_effects=True, vmem_limit_bytes=56 * 2**20
        ),
    )(
        valid_rows,
        list_owner.T,
        list_slot.reshape(1, -1),
        pq_codes.T,
        memory_rows,
        centroids,
        codebook.transpose(0, 2, 1),
    )
    newcb, err = pl.pallas_call(
        hand_over,
        out_shape=(
            jax.ShapeDtypeStruct((2, DS, K), F32),
            jax.ShapeDtypeStruct((1, ROWS), F32),
        ),
        in_specs=[vmem, vmem],
        out_specs=(vmem, vmem),
    )(newcb, err)
    return newcb.transpose(0, 2, 1), err.reshape(-1)


def solution(mesh):
    in_specs = (
        P(("list", "rep"), None),
        P(("list", "rep"), None),
        P(("list", "rep")),
        P(("list", "rep"), None),
        P(("list", "rep")),
        P("list", None),
        P(),
    )
    out_specs = (P("rep", None, None), P(("list", "rep")))
    return jax.shard_map(body, mesh=mesh, in_specs=in_specs, out_specs=out_specs, check_vma=False)
```
